256 devices in a mesh: section: 16 (over y, x_hi, core), peer: 16 (over x_lo, z).
Axes of the slice: x: 4 (x_hi: 2, x_lo: 2; x = x_hi * 2 + x_lo), y: 4, z: 8, core: 2. Of those that a mesh axis runs over, the one named last changes fastest.
Arguments:
- inputs: bfloat16 [16, 16, 128, 5120], P('section', 'peer'), may hold values from -6 to 6
- out_grad: bfloat16 [16, 16, 128, 5120], P('section', 'peer'), may hold values from -6 to 6
- gains: float32 [16, 5120], P('section'), may hold values from 0.1 to 1.9
- down_proj: bfloat16 [16, 5120, 128], P('section'), may hold values from -0.078125 to 0.078125
- up_proj: bfloat16 [16, 128, 5120], P('section'), may hold values from -0.5 to 0.5
- wiring: int32 [16, 16, 16], replicated, may hold values from 0 to 2, as said below
- pair_mask: int32 [16], replicated, may hold values from 1 to 15
Outputs:
- next_inputs: bfloat16 [16, 16, 128, 5120], P('section', 'peer')
- returned_grad: bfloat16 [16, 16, 128, 5120], P('section', 'peer')
- grad_down: float32 [16, 16, 5120, 128], P('section', 'peer')
- grad_up: float32 [16, 16, 128, 5120], P('section', 'peer')
The draws below stay inside these ranges and needn't reach their ends.
Inputs may be any that keep to these rules, and one draw needn't show every extreme that they name: For each section, every row and every column of wiring sums to 16; entries are 0, 1 or 2, and 2 occurs in every row and every column. `pair_mask`: 16 is a power of two; each section's mask is nonzero.
All inputs are finite; a program needn't handle non-finite values.
Results may differ from the reference program's by a relative error of at most 0.006.
Values may be sent and summed in bfloat16 or wider, within the bound.
A program may use at most 128 MiB of HBM per device.

```python
import jax
import jax.numpy as jnp
from jax import lax

D = 5120
R = 128
TOK = 128
NB = 16
BLK = 8
SECTIONS = 16
PEERS = 16


def draw_wiring(key, part):
    keys = jax.random.split(jax.random.fold_in(key, 17), SECTIONS)

    def one_section(section_key):
        key_a, key_b = jax.random.split(section_key)
        order = jax.random.permutation(key_a, PEERS)
        shifts = jax.random.permutation(key_b, PEERS)
        rows = jnp.arange(PEERS, dtype=jnp.int32)
        cols = jnp.arange(PEERS, dtype=jnp.int32)
        total = jnp.zeros((PEERS, PEERS), jnp.int32)
        heavy = PEERS // 4
        light = PEERS // 2
        for index in range(heavy + light):
            weight = 2 if index < heavy else 1
            target = order[(rows + shifts[index]) % PEERS]
            total = total + weight * (target[:, None] == cols[None, :]).astype(jnp.int32)
        return total
    return jax.vmap(one_section)(keys).astype(jnp.int32)


def place_ends(drawn, stream_key, smallest, top_value):
    extent = drawn.shape
    spot = [jax.random.randint(jax.random.fold_in(stream_key, axis), (), 0, extent[axis]) for axis in range(len(extent))]
    drawn = drawn.at[tuple(spot)].set(smallest)
    longest = extent.index(max(extent))
    spot[longest] = (spot[longest] + 1) % extent[longest]
    return drawn.at[tuple(spot)].set(top_value)


def levels(rng, shape, cuts, least, high):
    level, own = 1.0, jax.random.fold_in(rng, 6)
    for dim, blocks in cuts:
        heights = jnp.exp(jax.random.uniform(jax.random.fold_in(own, dim), (blocks,), jnp.float32, least / len(cuts), high / len(cuts)))
        level = level * jnp.repeat(heights, shape[dim] // blocks).reshape([-1 if axis == dim else 1 for axis in range(len(shape))])
    return level


def noise(rng, dims, deviation, most, cuts=(), kind=jnp.bfloat16):
    loudness = levels(rng, dims, cuts, -0.22, 0.18) if cuts else 1.0
    values = jax.random.normal(rng, dims, jnp.float32) * deviation * loudness
    return jnp.minimum(jnp.maximum(values, -most), most).astype(kind)


def setup_inputs(seed: int = 0) -> dict:
    key_of = jax.random.split(jax.random.key(seed), 8)
    return {
        "inputs": noise(key_of[0], (SECTIONS, PEERS, TOK, D), 1.0, 6.0, ((0, 16), (1, 16))),
        "out_grad": noise(key_of[1], (SECTIONS, PEERS, TOK, D), 1.0, 6.0, ((0, 16), (1, 16))),
        "gains": jnp.clip(1.0 + 0.18 * jax.random.normal(key_of[2], (SECTIONS, D), jnp.float32), 0.1, 1.9),
        "down_proj": noise(key_of[3], (SECTIONS, D, R), D ** -0.5, 0.078125, ((0, 16),)),
        "up_proj": noise(key_of[4], (SECTIONS, R, D), R ** -0.5, 0.5, ((0, 16),)),
        "wiring": draw_wiring(jax.random.fold_in(key_of[7], 71), 0),
        "pair_mask": place_ends(jax.random.randint(key_of[6], (SECTIONS,), 1, PEERS), jax.random.fold_in(key_of[6], 1), 1, PEERS - 1).astype(jnp.int32),
    }


def layer(x, dy, g, down, up):
    xf = x.astype(jnp.float32)
    ms = lax.optimization_barrier(jnp.mean(xf * xf, axis=-1, keepdims=True))
    rinv = lax.rsqrt(ms + 1e-05)
    normed = (xf * rinv * g).astype(jnp.bfloat16)
    pre = jnp.dot(normed, down, preferred_element_type=jnp.float32)
    sig = jax.nn.sigmoid(pre)
    act = (pre * sig).astype(jnp.bfloat16)
    out = (xf + jnp.dot(act, up, preferred_element_type=jnp.float32)).astype(jnp.bfloat16)
    dact = lax.dot_general(dy, up, (((1,), (1,)), ((), ())), preferred_element_type=jnp.float32)
    dpre = (dact * sig * (1.0 + pre * (1.0 - sig))).astype(jnp.bfloat16)
    gup = lax.dot_general(act, dy, (((0,), (0,)), ((), ())), preferred_element_type=jnp.float32).astype(jnp.bfloat16)
    gdown = lax.dot_general(normed, dpre, (((0,), (0,)), ((), ())), preferred_element_type=jnp.float32).astype(jnp.bfloat16)
    dnorm = lax.dot_general(dpre, down, (((1,), (1,)), ((), ())), preferred_element_type=jnp.float32) * g
    inner = lax.optimization_barrier(jnp.mean(dnorm * xf, axis=-1, keepdims=True))
    dx = (dy.astype(jnp.float32) + rinv * (dnorm - xf * rinv * rinv * inner)).astype(jnp.bfloat16)
    return (out, dx, gdown, gup)

def destinations(counts):
    cum = jnp.cumsum(counts, axis=1)
    start = cum - counts
    colstart = jnp.cumsum(counts, axis=0) - counts
    blocks = jnp.arange(NB, dtype=jnp.int32)
    target = lax.optimization_barrier(jnp.sum((cum[:, None, :] <= blocks[None, :, None]).astype(jnp.int32), axis=2)).astype(jnp.int32)
    first = jnp.take_along_axis(start, target, axis=1)
    offset = jnp.take_along_axis(colstart, target, axis=1)
    dest = target * NB + offset + blocks[None, :] - first
    return dest.reshape(-1).astype(jnp.int32)

def reference(inputs, out_grad, gains, down_proj, up_proj, wiring, pair_mask):
    flat_x = inputs.reshape(SECTIONS * PEERS, TOK, D)
    flat_dy = out_grad.reshape(SECTIONS * PEERS, TOK, D)

    def single(index):
        section = index // PEERS
        return layer(flat_x[index], flat_dy[index], gains[section], down_proj[section], up_proj[section])
    outs, dxs, gdowns, gups = lax.map(single, jnp.arange(SECTIONS * PEERS, dtype=jnp.int32))
    out_blocks = outs.reshape(SECTIONS, PEERS * NB, BLK, D)
    dx_blocks = dxs.reshape(SECTIONS, PEERS * NB, BLK, D)
    dest = jax.vmap(destinations)(wiring)

    def place(where, blocks):
        return jnp.zeros_like(blocks).at[where].set(blocks)
    routed = jax.vmap(place)(dest, out_blocks)
    next_inputs = jnp.roll(routed, 1, axis=0).reshape(SECTIONS, PEERS, TOK, D)
    later = jnp.roll(dx_blocks, -1, axis=0)
    returned = jax.vmap(lambda where, blocks: blocks[where])(dest, later)
    returned_grad = returned.reshape(SECTIONS, PEERS, TOK, D)
    partner = jnp.bitwise_xor(jnp.arange(PEERS, dtype=jnp.int32)[None, :], pair_mask[:, None])
    gd = gdowns.reshape(SECTIONS, PEERS, D, R).astype(jnp.float32)
    gu = gups.reshape(SECTIONS, PEERS, R, D).astype(jnp.float32)
    gd_other = jnp.take_along_axis(gd, partner[:, :, None, None], axis=1)
    gu_other = jnp.take_along_axis(gu, partner[:, :, None, None], axis=1)
    return (next_inputs, returned_grad, (gd + gd_other) * 0.5, (gu + gu_other) * 0.5)
```

```python
import functools

import jax
import jax.numpy as jnp
from jax import lax
from jax.experimental import pallas as pl
from jax.experimental.pallas import tpu as pltpu
from jax.sharding import PartitionSpec as P

CAP = 2
MESH = pl.DeviceIdType.MESH
WIDE = 512


def layer_kernel(
    fslot, bslot, x_ref, dy_ref, g_ref, down_ref, up_ref,
    fwd_ref, back_ref, gup_ref, gdown_ref,
    normed, outs, dns, dxs, fsem, bsem,
):
    rows, width = x_ref.shape
    blocks, blk = outs.shape[0], outs.shape[1]
    rank = down_ref.shape[1]
    chunks = width // WIDE
    f32, bf16 = jnp.float32, jnp.bfloat16

    def cols(c):
        return pl.ds(pl.multiple_of(c * WIDE, WIDE), WIDE)

    def squares(c, total):
        xc = x_ref[:, cols(c)].astype(f32)
        return total + jnp.sum(xc * xc, axis=1, keepdims=True)

    ms = lax.fori_loop(0, chunks, squares, jnp.zeros((rows, 1), f32)) / width
    rinv = lax.rsqrt(ms + 1e-05)

    def project(c, carry):
        pre, dact = carry
        at = cols(c)
        nc = (x_ref[:, at].astype(f32) * rinv * g_ref[:, at]).astype(bf16)
        normed[:, at] = nc
        pre = pre + jnp.dot(nc, down_ref[at, :], preferred_element_type=f32)
        dact = dact + lax.dot_general(
            dy_ref[:, at], up_ref[:, at], (((1,), (1,)), ((), ())), preferred_element_type=f32
        )
        return pre, dact

    zero = jnp.zeros((rows, rank), f32)
    pre, dact = lax.fori_loop(0, chunks, project, (zero, zero))
    sig = jax.nn.sigmoid(pre)
    act = (pre * sig).astype(bf16)
    dpre = (dact * sig * (1.0 + pre * (1.0 - sig))).astype(bf16)

    def grads(c, inner):
        at = cols(c)
        xc = x_ref[:, at].astype(f32)
        gup_ref[:, at] = lax.dot_general(
            act, dy_ref[:, at], (((0,), (0,)), ((), ())), preferred_element_type=f32
        ).astype(bf16)
        gdown_ref[at, :] = lax.dot_general(
            normed[:, at], dpre, (((0,), (0,)), ((), ())), preferred_element_type=f32
        ).astype(bf16)
        oc = xc + jnp.dot(act, up_ref[:, at], preferred_element_type=f32)
        outs[:, :, at] = oc.reshape(blocks, blk, WIDE).astype(bf16)
        dn = (
            lax.dot_general(
                dpre, down_ref[at, :], (((1,), (1,)), ((), ())), preferred_element_type=f32
            )
            * g_ref[:, at]
        )
        dns[:, at] = dn
        return inner + jnp.sum(dn * xc, axis=1, keepdims=True)

    inner = lax.fori_loop(0, chunks, grads, jnp.zeros((rows, 1), f32)) / width

    def fwd_copy(i):
        return pltpu.make_async_copy(outs.at[fslot[i]], fwd_ref.at[i], fsem.at[i])

    def back_copy(i):
        return pltpu.make_async_copy(dxs.at[bslot[i]], back_ref.at[i], bsem.at[i])

    slots = fwd_ref.shape[0]
    pl.loop(0, slots)(lambda i: fwd_copy(i).start())
    pull = rinv * rinv * inner

    @pl.loop(0, chunks)
    def _(c):
        at = cols(c)
        xc = x_ref[:, at].astype(f32)
        dxc = dy_ref[:, at].astype(f32) + rinv * (dns[:, at] - xc * pull)
        dxs[:, :, at] = dxc.reshape(blocks, blk, WIDE).astype(bf16)

    pl.loop(0, slots)(lambda i: back_copy(i).start())
    pl.loop(0, slots)(lambda i: fwd_copy(i).wait())
    pl.loop(0, slots)(lambda i: back_copy(i).wait())


def layer(x, dy, g, down, up, fslot, bslot, blocks):
    rows, width = x.shape
    rank = down.shape[1]
    blk = rows // blocks
    vmem = pl.BlockSpec(memory_space=pltpu.VMEM)
    smem = pl.BlockSpec(memory_space=pltpu.SMEM)
    hbm = pl.BlockSpec(memory_space=pl.ANY)
    slots = blocks * CAP
    bf16 = jnp.bfloat16
    return pl.pallas_call(
        layer_kernel,
        name="adapter",
        in_specs=[smem, smem, vmem, vmem, vmem, vmem, vmem],
        out_specs=[hbm, hbm, vmem, vmem],
        out_shape=[
            jax.ShapeDtypeStruct((slots, blk, width), bf16),
            jax.ShapeDtypeStruct((slots, blk, width), bf16),
            jax.ShapeDtypeStruct((rank, width), bf16),
            jax.ShapeDtypeStruct((width, rank), bf16),
        ],
        scratch_shapes=[
            pltpu.VMEM((rows, width), bf16),
            pltpu.VMEM((blocks, blk, width), bf16),
            pltpu.VMEM((rows, width), jnp.float32),
            pltpu.VMEM((blocks, blk, width), bf16),
            pltpu.SemaphoreType.DMA((slots,)),
            pltpu.SemaphoreType.DMA((slots,)),
        ],
    )(fslot, bslot, x, dy, g, down, up)


def exchange_kernel(
    sections, peers, mask_ref, fwd, back, up, down,
    fwd_out, back_out, up_out, down_out,
    up_got, down_got, up_send, down_send,
    sems_f, sems_b, sems_u, sems_d, sems_u2, sems_d2, own_sem,
):
    section = lax.axis_index("section")
    me = lax.axis_index("peer")
    after = lax.rem(section + 1, sections)
    ahead = lax.rem(section + sections - 1, sections)

    def turn(t):
        half = (t + 1) // 2
        step = half + (1 - t % 2) * (peers - 2 * half)
        return lax.rem(me + step, peers)

    barrier = pltpu.get_barrier_semaphore()

    @pl.loop(0, peers)
    def _(t):
        who = turn(t)
        for where in (after, ahead):
            pl.semaphore_signal(
                barrier, inc=1, device_id={"section": where, "peer": who}, device_id_type=MESH
            )

    @pl.loop(1, peers)
    def _(t):
        pl.semaphore_signal(
            barrier, inc=1, device_id={"section": section, "peer": turn(t)}, device_id_type=MESH
        )

    pl.semaphore_wait(barrier, 3 * peers - 1)

    def remote(src, dst, sems, where, who):
        return pltpu.make_async_remote_copy(
            src_ref=src.at[who],
            dst_ref=dst.at[me],
            send_sem=sems.at[0, who],
            recv_sem=sems.at[1, me],
            device_id={"section": where, "peer": who},
            device_id_type=MESH,
        )

    def arrival(src, dst, sems, where, who):
        return pltpu.make_async_remote_copy(
            src_ref=src.at[who],
            dst_ref=dst.at[who],
            send_sem=sems.at[0, who],
            recv_sem=sems.at[1, who],
            device_id={"section": where, "peer": who},
            device_id_type=MESH,
        )

    own = (
        pltpu.make_async_copy(up.at[me], up_got.at[me], own_sem.at[0]),
        pltpu.make_async_copy(down.at[me], down_got.at[me], own_sem.at[1]),
    )
    for copy in own:
        copy.start()

    @pl.loop(1, peers)
    def _(t):
        who = turn(t)
        remote(up, up_got, sems_u, section, who).start()
        remote(down, down_got, sems_d, section, who).start()

    @pl.loop(0, peers)
    def _(t):
        who = turn(t)
        remote(fwd, fwd_out, sems_f, after, who).start()
        remote(back, back_out, sems_b, ahead, who).start()

    for copy in own:
        copy.wait()

    @pl.loop(1, peers)
    def _(t):
        who = turn(t)
        arrival(up, up_got, sems_u, section, who).wait_recv()
        arrival(down, down_got, sems_d, section, who).wait_recv()

    mask = mask_ref[0]

    @pl.loop(0, peers)
    def _(p):
        pair = jnp.bitwise_xor(p, mask)
        up_send[p] = up_got[pair]
        down_send[p] = down_got[pair]

    @pl.loop(1, peers)
    def _(t):
        who = turn(t)
        remote(up_send, up_out, sems_u2, section, who).start()
        remote(down_send, down_out, sems_d2, section, who).start()

    back_home = (
        pltpu.make_async_copy(up_send.at[me], up_out.at[me], own_sem.at[2]),
        pltpu.make_async_copy(down_send.at[me], down_out.at[me], own_sem.at[3]),
    )
    for copy in back_home:
        copy.start()

    @pl.loop(1, peers)
    def _(t):
        who = turn(t)
        remote(up, up_got, sems_u, section, who).wait_send()
        remote(down, down_got, sems_d, section, who).wait_send()

    @pl.loop(0, peers)
    def _(t):
        who = turn(t)
        remote(fwd, fwd_out, sems_f, after, who).wait_send()
        remote(back, back_out, sems_b, ahead, who).wait_send()
        arrival(fwd, fwd_out, sems_f, after, who).wait_recv()
        arrival(back, back_out, sems_b, ahead, who).wait_recv()

    for copy in back_home:
        copy.wait()

    @pl.loop(1, peers)
    def _(t):
        who = turn(t)
        remote(up_send, up_out, sems_u2, section, who).wait_send()
        remote(down_send, down_out, sems_d2, section, who).wait_send()
        arrival(up_send, up_out, sems_u2, section, who).wait_recv()
        arrival(down_send, down_out, sems_d2, section, who).wait_recv()


def exchange(mask, fwd, back, up, down, sections, peers):
    smem = pl.BlockSpec(memory_space=pltpu.SMEM)
    hbm = pl.BlockSpec(memory_space=pl.ANY)
    like = lambda a: jax.ShapeDtypeStruct(a.shape, a.dtype)
    dma = pltpu.SemaphoreType.DMA
    return pl.pallas_call(
        functools.partial(exchange_kernel, sections, peers),
        name="exchange",
        in_specs=[smem, hbm, hbm, hbm, hbm],
        out_specs=[hbm] * 4,
        out_shape=[like(fwd), like(back), like(up), like(down)],
        scratch_shapes=[
            pltpu.VMEM(up.shape, up.dtype),
            pltpu.VMEM(down.shape, down.dtype),
            pltpu.VMEM(up.shape, up.dtype),
            pltpu.VMEM(down.shape, down.dtype),
        ]
        + [dma((2, peers))] * 6
        + [dma((4,))],
        compiler_params=pltpu.CompilerParams(collective_id=0, has_side_effects=True),
    )(mask, fwd, back, up, down)


def settle_kernel(
    fpick, bpick, fwd, back, up, down, up_other, down_other, next_ref, ret_ref, gdown, gup
):
    f32 = jnp.float32
    next_ref[...] = fwd[...]
    ret_ref[...] = back[...]
    gup[...] = (up[...].astype(f32) + up_other[...].astype(f32)) * 0.5
    gdown[...] = (down[...].astype(f32) + down_other[...].astype(f32)) * 0.5


def settle(fpick, bpick, fwd, back, up, down, up_other, down_other):
    blocks, blk, width = up.shape
    deep, rank = down.shape[1:]
    rows_in = lambda pick: (1, blk, width)
    row = pl.BlockSpec((1, blk, width), lambda i, f, b: (i, 0, 0))
    deep_row = pl.BlockSpec((1, deep, rank), lambda i, f, b: (i, 0, 0))
    return pl.pallas_call(
        settle_kernel,
        name="settle",
        grid_spec=pltpu.PrefetchScalarGridSpec(
            num_scalar_prefetch=2,
            grid=(blocks,),
            in_specs=[
                pl.BlockSpec((1, blk, width), lambda i, f, b: (f[i], 0, 0)),
                pl.BlockSpec((1, blk, width), lambda i, f, b: (b[i], 0, 0)),
                row,
                deep_row,
                row,
                deep_row,
            ],
            out_specs=[row, row, deep_row, row],
        ),
        out_shape=[
            jax.ShapeDtypeStruct((blocks, blk, width), fwd.dtype),
            jax.ShapeDtypeStruct((blocks, blk, width), back.dtype),
            jax.ShapeDtypeStruct((blocks, deep, rank), jnp.float32),
            jax.ShapeDtypeStruct((blocks, blk, width), jnp.float32),
        ],
    )(fpick, bpick, fwd, back, up, down, up_other, down_other)


def tables(counts):
    n = counts.shape[0]
    order = jnp.arange(n, dtype=jnp.int32)
    start = jnp.sum(jnp.where(order[None, :] < order[:, None], counts[None, :], 0), axis=1)
    slot = jnp.minimum(start[:, None] + jnp.arange(CAP, dtype=jnp.int32)[None, :], n - 1)
    inside = (order[:, None] >= start[None, :]) & (order[:, None] < (start + counts)[None, :])
    place = order[None, :] * CAP + order[:, None] - start[None, :]
    pick = jnp.sum(jnp.where(inside, place, 0), axis=1)
    return slot.reshape(-1).astype(jnp.int32), pick.astype(jnp.int32)


def body(inputs, out_grad, gains, down_proj, up_proj, wiring, pair_mask):
    sections = lax.axis_size("section")
    peers = lax.axis_size("peer")
    section = lax.axis_index("section")
    peer = lax.axis_index("peer")
    x = inputs[0, 0]
    rows, width = x.shape
    rank = down_proj.shape[2]
    blk = rows // peers
    here = lax.dynamic_slice(wiring, (section, peer, 0), (1, 1, peers)).reshape(peers)
    before = lax.dynamic_slice(
        wiring, (lax.rem(section + sections - 1, sections), 0, peer), (1, peers, 1)
    ).reshape(peers)
    mask = lax.dynamic_slice(pair_mask, (section,), (1,))
    fslot, bpick = tables(here)
    bslot, fpick = tables(before)
    fwd, back, up, down = layer(
        x, out_grad[0, 0], gains, down_proj[0], up_proj[0], fslot, bslot, peers
    )
    up = up.reshape(peers, rank // peers, width)
    down = down.reshape(peers, width // peers, rank)
    shape = (peers, CAP, blk, width)
    got_fwd, got_back, up_other, down_other = exchange(
        mask, fwd.reshape(shape), back.reshape(shape), up, down, sections, peers
    )
    flat = (peers * CAP, blk, width)
    next_rows, return_rows, grad_down, grad_up = settle(
        fpick, bpick, got_fwd.reshape(flat), got_back.reshape(flat), up, down, up_other, down_other
    )
    return (
        next_rows.reshape(1, 1, rows, width),
        return_rows.reshape(1, 1, rows, width),
        grad_down.reshape(1, 1, width, rank),
        grad_up.reshape(1, 1, rank, width),
    )


def solution(mesh):
    placed = (
        P("section", "peer", None, None),
        P("section", "peer", None, None),
        P("section", None),
        P("section", None, None),
        P("section", None, None),
        P(),
        P(),
    )
    return jax.shard_map(
        body,
        mesh=mesh,
        in_specs=placed,
        out_specs=(
            P("section", "peer", None, None),
            P("section", "peer", None, None),
            P("section", "peer", None, None),
            P("section", "peer", None, None),
        ),
        check_vma=False,
    )
```

```python
import functools

import jax
import jax.numpy as jnp
from jax import lax
from jax.experimental import pallas as pl
from jax.experimental.pallas import tpu as pltpu
from jax.sharding import PartitionSpec as P

CAP = 2
WIDE = 512
PARTS = 4
MESH = pl.DeviceIdType.MESH
F32, BF16 = jnp.float32, jnp.bfloat16


def dims(a, b):
    return (((a,), (b,)), ((), ()))


def section_kernel(
    sections, peers, masks, g_ref, wiring, x_hbm, dy_hbm, down_hbm, up_hbm,
    fwd_out, back_out, gup_out, gdown_out, gup2_out, gdown2_out,
    x_own, dy_own, down_ref, up_ref, x_got, dy_got, x_send, dy_send, x_pair, dy_pair,
    normed, dns, outs, dxs, fwd, back, gup, gdown, gup2, gdown2, counts,
    load_sem, own_sem, out_sem, x1, dy1, x2, dy2, sems_f, sems_b,
):
    section = lax.axis_index("section")
    me = lax.axis_index("peer")
    after = lax.rem(section + 1, sections)
    ahead = lax.rem(section + sections - 1, sections)
    blocks, blk, width = x_own.shape
    rows = blocks * blk
    rank = up_ref.shape[0]
    chunks = width // WIDE

    def turn(t):
        half = (t + 1) // 2
        step = half + (1 - t % 2) * (peers - 2 * half)
        return lax.rem(me + step, peers)

    loads = [
        pltpu.make_async_copy(src, dst, load_sem.at[i])
        for i, (src, dst) in enumerate((
            (x_hbm, x_own),
            (dy_hbm, dy_own),
            (down_hbm, down_ref),
            (up_hbm, up_ref),
            (wiring.at[section], counts.at[0]),
            (wiring.at[ahead], counts.at[1]),
            (x_hbm.at[me], x_got.at[me]),
            (dy_hbm.at[me], dy_got.at[me]),
        ))
    ]
    for copy in loads:
        copy.start()

    barrier = pltpu.get_barrier_semaphore()

    @pl.loop(0, peers)
    def _(t):
        who = turn(t)
        for where in (after, ahead):
            pl.semaphore_signal(
                barrier, inc=1, device_id={"section": where, "peer": who}, device_id_type=MESH
            )

    @pl.loop(1, peers)
    def _(t):
        pl.semaphore_signal(
            barrier, inc=1, device_id={"section": section, "peer": turn(t)}, device_id_type=MESH
        )

    pl.semaphore_wait(barrier, 3 * peers - 1)

    def remote(src, dst, sems, where, who):
        return pltpu.make_async_remote_copy(
            src_ref=src.at[who],
            dst_ref=dst.at[me],
            send_sem=sems.at[0, who],
            recv_sem=sems.at[1, me],
            device_id={"section": where, "peer": who},
            device_id_type=MESH,
        )

    def arrival(src, dst, sems, where, who):
        return pltpu.make_async_remote_copy(
            src_ref=src.at[who],
            dst_ref=dst.at[who],
            send_sem=sems.at[0, who],
            recv_sem=sems.at[1, who],
            device_id={"section": where, "peer": who},
            device_id_type=MESH,
        )

    @pl.loop(1, peers)
    def _(t):
        who = turn(t)
        remote(x_hbm, x_got, x1, section, who).start()
        remote(dy_hbm, dy_got, dy1, section, who).start()

    for copy in loads:
        copy.wait()

    def cols(c):
        return pl.ds(pl.multiple_of(c * WIDE, WIDE), WIDE)

    def wide(ref, at):
        return ref[:, :, at].astype(F32).reshape(rows, WIDE)

    def tall(value):
        return value.reshape(blocks, blk, WIDE).astype(BF16)

    def head(x_ref, dy_ref):
        def squares(c, total):
            xc = wide(x_ref, cols(c))
            return total + jnp.sum(xc * xc, axis=1, keepdims=True)

        ms = lax.fori_loop(0, chunks, squares, jnp.zeros((rows, 1), F32)) / width
        rinv = lax.rsqrt(ms + 1e-05)

        def project(c, carry):
            pre, dact = carry
            at = cols(c)
            nc = (wide(x_ref, at) * rinv * g_ref[:, at]).astype(BF16)
            normed[:, at] = nc
            pre = pre + jnp.dot(nc, down_ref[at, :], preferred_element_type=F32)
            dact = dact + lax.dot_general(
                wide(dy_ref, at).astype(BF16), up_ref[:, at], dims(1, 1), preferred_element_type=F32
            )
            return pre, dact

        zero = jnp.zeros((rows, rank), F32)
        pre, dact = lax.fori_loop(0, chunks, project, (zero, zero))
        sig = jax.nn.sigmoid(pre)
        act = (pre * sig).astype(BF16)
        dpre = (dact * sig * (1.0 + pre * (1.0 - sig))).astype(BF16)
        return rinv, act, dpre

    def gradients(at, dy_ref, act, dpre, up_to, down_to):
        up_to[:, :, at] = tall(
            lax.dot_general(
                act, wide(dy_ref, at).astype(BF16), dims(0, 0), preferred_element_type=F32
            )
        )
        down_to[at, :] = lax.dot_general(
            normed[:, at], dpre, dims(0, 0), preferred_element_type=F32
        ).astype(BF16)

    rinv, act, dpre = head(x_own, dy_own)

    def tail(c, inner):
        at = cols(c)
        xc = wide(x_own, at)
        outs[:, :, at] = tall(xc + jnp.dot(act, up_ref[:, at], preferred_element_type=F32))
        dn = (
            lax.dot_general(dpre, down_ref[at, :], dims(1, 1), preferred_element_type=F32)
            * g_ref[:, at]
        )
        dns[:, at] = dn
        gradients(at, dy_own, act, dpre, gup, gdown)
        return inner + jnp.sum(dn * xc, axis=1, keepdims=True)

    inner = lax.fori_loop(0, chunks, tail, jnp.zeros((rows, 1), F32)) / width
    pull = rinv * rinv * inner

    @pl.loop(0, chunks)
    def _(c):
        at = cols(c)
        dxs[:, :, at] = tall(wide(dy_own, at) + rinv * (dns[:, at] - wide(x_own, at) * pull))

    def spread(source, target, count):
        def one(q, start):
            for slot in range(CAP):
                target[q, slot] = source[jnp.minimum(start + slot, blocks - 1)]
            return start + count(q)

        lax.fori_loop(0, peers, one, jnp.int32(0))

    spread(dxs, back, lambda q: counts[1, q, me])

    @pl.loop(0, peers)
    def _(t):
        remote(back, back_out, sems_b, ahead, turn(t)).start()

    spread(outs, fwd, lambda q: counts[0, me, q])
    saves = [
        pltpu.make_async_copy(gup, gup_out, out_sem.at[0]),
        pltpu.make_async_copy(gdown, gdown_out, out_sem.at[1]),
    ]
    for copy in saves:
        copy.start()

    mask = masks[section]

    @pl.loop(1, peers)
    def _(t):
        who = turn(t)
        arrival(x_hbm, x_got, x1, section, who).wait_recv()
        arrival(dy_hbm, dy_got, dy1, section, who).wait_recv()

    @pl.loop(0, peers)
    def _(p):
        pair = jnp.bitwise_xor(p, mask)
        x_send[p] = x_got[pair]
        dy_send[p] = dy_got[pair]

    @pl.loop(1, peers)
    def _(t):
        who = turn(t)
        remote(x_send, x_pair, x2, section, who).start()
        remote(dy_send, dy_pair, dy2, section, who).start()

    kept = [
        pltpu.make_async_copy(x_send.at[me], x_pair.at[me], own_sem.at[0]),
        pltpu.make_async_copy(dy_send.at[me], dy_pair.at[me], own_sem.at[1]),
    ]
    for copy in kept:
        copy.start()

    @pl.loop(0, peers)
    def _(t):
        remote(fwd, fwd_out, sems_f, after, turn(t)).start()

    for copy in kept:
        copy.wait()

    @pl.loop(1, peers)
    def _(t):
        who = turn(t)
        arrival(x_send, x_pair, x2, section, who).wait_recv()
        arrival(dy_send, dy_pair, dy2, section, who).wait_recv()

    _, act2, dpre2 = head(x_pair, dy_pair)

    @pl.loop(0, chunks)
    def _(c):
        gradients(cols(c), dy_pair, act2, dpre2, gup2, gdown2)

    saves += [
        pltpu.make_async_copy(gup2, gup2_out, out_sem.at[2]),
        pltpu.make_async_copy(gdown2, gdown2_out, out_sem.at[3]),
    ]
    for copy in saves[2:]:
        copy.start()

    @pl.loop(1, peers)
    def _(t):
        who = turn(t)
        remote(x_hbm, x_got, x1, section, who).wait_send()
        remote(dy_hbm, dy_got, dy1, section, who).wait_send()
        remote(x_send, x_pair, x2, section, who).wait_send()
        remote(dy_send, dy_pair, dy2, section, who).wait_send()

    @pl.loop(0, peers)
    def _(t):
        who = turn(t)
        remote(fwd, fwd_out, sems_f, after, who).wait_send()
        remote(back, back_out, sems_b, ahead, who).wait_send()
        arrival(fwd, fwd_out, sems_f, after, who).wait_recv()
        arrival(back, back_out, sems_b, ahead, who).wait_recv()

    for copy in saves:
        copy.wait()


def run_section(masks, g, wiring, x, dy, down, up, sections, peers):
    vmem = pl.BlockSpec(memory_space=pltpu.VMEM)
    smem = pl.BlockSpec(memory_space=pltpu.SMEM)
    hbm = pl.BlockSpec(memory_space=pl.ANY)
    dma = pltpu.SemaphoreType.DMA
    blocks, blk, width = x.shape
    rows, rank = blocks * blk, up.shape[0]
    piece = pltpu.VMEM(x.shape, BF16)
    slots = (peers, CAP, blk, width)
    up3 = (peers, rank // peers, width)
    return pl.pallas_call(
        functools.partial(section_kernel, sections, peers),
        name="section_layer",
        in_specs=[smem, vmem] + [hbm] * 5,
        out_specs=[hbm] * 6,
        out_shape=[
            jax.ShapeDtypeStruct(slots, BF16),
            jax.ShapeDtypeStruct(slots, BF16),
            jax.ShapeDtypeStruct(up3, BF16),
            jax.ShapeDtypeStruct(down.shape, BF16),
            jax.ShapeDtypeStruct(up3, BF16),
            jax.ShapeDtypeStruct(down.shape, BF16),
        ],
        scratch_shapes=[
            piece, piece, pltpu.VMEM(down.shape, BF16), pltpu.VMEM(up.shape, BF16),
            piece, piece, piece, piece, piece, piece,
            pltpu.VMEM((rows, width), BF16), pltpu.VMEM((rows, width), F32),
            piece, piece, pltpu.VMEM(slots, BF16), pltpu.VMEM(slots, BF16),
            pltpu.VMEM(up3, BF16), pltpu.VMEM(down.shape, BF16),
            pltpu.VMEM(up3, BF16), pltpu.VMEM(down.shape, BF16),
            pltpu.SMEM((2, peers, peers), jnp.int32),
            dma((8,)), dma((2,)), dma((4,)),
        ]
        + [dma((2, peers))] * 6,
        compiler_params=pltpu.CompilerParams(
            collective_id=0, has_side_effects=True, vmem_limit_bytes=60 * 1024 * 1024
        ),
    )(masks, g, wiring, x, dy, down, up)


def settle_kernel(
    sections, wiring, fwd, back, up, down, up2, down2,
    next_out, ret_out, gdown_out, gup_out,
    counts, nexts, rets, ups, downs, up2s, down2s, gups, gdowns,
    count_sem, row_sem, read_sem, write_sem,
):
    section = lax.axis_index("section")
    me = lax.axis_index("peer")
    ahead = lax.rem(section + sections - 1, sections)
    tables = [
        pltpu.make_async_copy(wiring.at[section], counts.at[0], count_sem.at[0]),
        pltpu.make_async_copy(wiring.at[ahead], counts.at[1], count_sem.at[1]),
    ]
    for copy in tables:
        copy.start()
    peers = counts.shape[1]

    def part(ref, c):
        size = ref.shape[0] // PARTS
        return ref.at[pl.ds(c * size, size)]

    pairs = ((up, ups), (up2, up2s), (down, downs), (down2, down2s))
    reads = [
        [
            pltpu.make_async_copy(part(src, c), part(dst, c), read_sem.at[c, i])
            for i, (src, dst) in enumerate(pairs)
        ]
        for c in range(PARTS)
    ]
    for copy in reads[0]:
        copy.start()
    for copy in tables:
        copy.wait()

    def gather(p, starts):
        moved = []
        for k, (source, target, n) in enumerate(
            ((fwd, nexts, counts[1, p, me]), (back, rets, counts[0, me, p]))
        ):
            for slot in range(CAP):
                @pl.when(slot < n)
                def _():
                    at = starts[k] + slot
                    pltpu.make_async_copy(
                        source.at[p, slot], target.at[at], row_sem.at[k, at]
                    ).start()

            moved.append(starts[k] + n)
        return tuple(moved)

    lax.fori_loop(0, peers, gather, (jnp.int32(0), jnp.int32(0)))
    for group in reads[1:]:
        for copy in group:
            copy.start()

    writes = []
    for c in range(PARTS):
        for copy in reads[c]:
            copy.wait()
        for a, b, total, out, i in (
            (ups, up2s, gups, gup_out, 0),
            (downs, down2s, gdowns, gdown_out, 1),
        ):
            size = a.shape[0] // PARTS
            at = pl.ds(c * size, size)
            total[at] = (a[at].astype(F32) + b[at].astype(F32)) * 0.5
            writes.append(
                pltpu.make_async_copy(part(total, c), part(out, c), write_sem.at[c, i])
            )
            writes[-1].start()

    for k, (source, target, out) in enumerate(((fwd, nexts, next_out), (back, rets, ret_out))):
        @pl.loop(0, peers)
        def _(b):
            pltpu.make_async_copy(source.at[0, 0], target.at[b], row_sem.at[k, b]).wait()

        writes.append(pltpu.make_async_copy(target, out, write_sem.at[PARTS, k]))
        writes[-1].start()
    for copy in writes:
        copy.wait()


def settle(wiring, fwd, back, up, down, up2, down2, sections):
    hbm = pl.BlockSpec(memory_space=pl.ANY)
    dma = pltpu.SemaphoreType.DMA
    peers, _, blk, width = fwd.shape
    rows = (peers, blk, width)
    return pl.pallas_call(
        functools.partial(settle_kernel, sections),
        name="settle",
        in_specs=[hbm] * 7,
        out_specs=[hbm] * 4,
        out_shape=[
            jax.ShapeDtypeStruct(rows, BF16),
            jax.ShapeDtypeStruct(rows, BF16),
            jax.ShapeDtypeStruct(down.shape, F32),
            jax.ShapeDtypeStruct(up.shape, F32),
        ],
        scratch_shapes=[
            pltpu.SMEM((2, peers, peers), jnp.int32),
            pltpu.VMEM(rows, BF16), pltpu.VMEM(rows, BF16),
            pltpu.VMEM(up.shape, BF16), pltpu.VMEM(down.shape, BF16),
            pltpu.VMEM(up.shape, BF16), pltpu.VMEM(down.shape, BF16),
            pltpu.VMEM(up.shape, F32), pltpu.VMEM(down.shape, F32),
            dma((2,)), dma((2, peers)), dma((PARTS, 4)), dma((PARTS + 1, 2)),
        ],
    )(wiring, fwd, back, up, down, up2, down2)


def body(inputs, out_grad, gains, down_proj, up_proj, wiring, pair_mask):
    sections = lax.axis_size("section")
    peers = lax.axis_size("peer")
    rows, width = inputs.shape[2:]
    rank = down_proj.shape[2]
    pieces = (peers, rows // peers, width)
    fwd, back, up, down, up2, down2 = run_section(
        pair_mask, gains, wiring, inputs.reshape(pieces), out_grad.reshape(pieces),
        down_proj[0], up_proj[0], sections, peers,
    )
    next_rows, return_rows, grad_down, grad_up = settle(
        wiring, fwd, back, up, down, up2, down2, sections
    )
    return (
        next_rows.reshape(1, 1, rows, width),
        return_rows.reshape(1, 1, rows, width),
        grad_down.reshape(1, 1, width, rank),
        grad_up.reshape(1, 1, rank, width),
    )


def solution(mesh):
    placed = (
        P("section", "peer", None, None),
        P("section", "peer", None, None),
        P("section", None),
        P("section", None, None),
        P("section", None, None),
        P(),
        P(),
    )
    return jax.shard_map(
        body,
        mesh=mesh,
        in_specs=placed,
        out_specs=(
            P("section", "peer", None, None),
            P("section", "peer", None, None),
            P("section", "peer", None, None),
            P("section", "peer", None, None),
        ),
        check_vma=False,
    )
```

```python
import functools

import jax
import jax.numpy as jnp
from jax import lax
from jax.experimental import pallas as pl
from jax.experimental.pallas import tpu as pltpu
from jax.sharding import PartitionSpec as P

CAP = 2
WIDE = 512
PARTS = 4
EARLY = 8
MESH = pl.DeviceIdType.MESH
F32, BF16 = jnp.float32, jnp.bfloat16


def dims(a, b):
    return (((a,), (b,)), ((), ()))


def mul(a, b, ca=1, cb=0):
    return lax.dot_general(a, b, dims(ca, cb), preferred_element_type=F32)


def hot(mask):
    return mask.astype(F32).astype(BF16)


def iota(shape, dim):
    return lax.broadcasted_iota(jnp.int32, shape, dim)


def block_graph(counts):
    n = counts.shape[0]
    e, bits = n * n, n.bit_length() - 1
    c = counts.astype(BF16)
    start = mul(c, hot(iota((n, n), 0) < iota((n, n), 1)))
    above = mul(hot(iota((n, n), 1) < iota((n, n), 0)), c)
    right = hot((iota((e, n), 0) >> bits) == iota((e, n), 1))
    left = hot((iota((n, e), 1) >> bits) == iota((n, e), 0))

    def grow(m):
        return mul(mul(right, m.astype(BF16), 1, 1).astype(BF16), left)

    rank = (iota((e, e), 1) & (n - 1)).astype(F32) - grow(start)
    place = (iota((e, e), 0) & (n - 1)).astype(F32)
    inside = (rank >= 0) & (rank < grow(counts)) & (place == grow(above) + rank)
    return hot(inside)


def halve(graph, left, right, size):
    e = graph.shape[0]
    row, col = iota((e, e), 0), iota((e, e), 1)
    swap = hot((row >> 1 == col >> 1) & (row != col))
    mate = mul(graph, mul(swap, graph).astype(BF16), 0, 0).astype(BF16)
    step = mul(mate, swap).astype(BF16)

    def jump(_, carry):
        low, step = carry
        low = jnp.minimum(low, mul(low.astype(BF16), step))
        return low, mul(step, step).astype(BF16)

    longest = e * size >> (e.bit_length() - 1) // 2 + 1
    low, _ = lax.fori_loop(0, longest.bit_length() - 1, jump, (iota((8, e), 1).astype(F32), step))
    side = (low > mul(low.astype(BF16), swap)).astype(F32)
    at = iota((8, e), 1)
    base = ((at & ~(size - 1)) + ((at & (size - 1)) >> 1)).astype(F32)

    def moved(half):
        return hot(row.astype(F32) == (base + half * (size // 2))[0:1, :])

    on_left, on_right = moved(side), moved(mul(side.astype(BF16), graph, 1, 1))
    graph = mul(mul(on_right, graph).astype(BF16), on_left, 1, 1).astype(BF16)
    return graph, mul(on_left, left).astype(BF16), mul(on_right, right).astype(BF16)


def colours(counts):
    graph = block_graph(counts)
    size, e = counts.shape[0], graph.shape[0]
    left = right = hot(iota((e, e), 0) == iota((e, e), 1))
    while size > 1:
        graph, left, right = halve(graph, left, right, size)
        size //= 2
    return graph, left, right


def cut(matrix, blocks, blk, rows_at, cols_at):
    e, n, bits = matrix.shape[0], blocks * blk, blk.bit_length() - 1
    pick = hot(iota((n, e), 1) == rows_at(iota((n, e), 0) >> bits))
    take = hot(iota((e, n), 0) == cols_at(iota((e, n), 1) >> bits))
    found = mul(mul(pick, matrix).astype(BF16), take)
    same = (iota((n, n), 0) & (blk - 1)) == (iota((n, n), 1) & (blk - 1))
    return hot(same & (found > 0.5))


def section_kernel(
    sections, peers, masks, g_ref, wiring, x_hbm, dy_hbm, down_hbm, up_hbm,
    fwd_out, back_out, gup_out, gdown_out, gup2_out, gdown2_out, place_out,
    x_own, dy_own, down_ref, up_ref, x_pack, x_got, dy_got, x_send, dy_send, x_pair, dy_pair,
    x_flat, normed, dns, dxs, fwd, back, gup, gdown, gup2, gdown2, graph_ref, left_ref,
    counts, tables, load_sem, own_sem, out_sem, x1, dy1, x2, dy2, sems_f, sems_b,
):
    section = lax.axis_index("section")
    me = lax.axis_index("peer")
    after = lax.rem(section + 1, sections)
    ahead = lax.rem(section + sections - 1, sections)
    blocks, blk, width = x_own.shape
    rows = blocks * blk
    rank = up_ref.shape[0]
    chunks = width // WIDE

    def turn(t):
        half = (t + 1) // 2
        step = half + (1 - t % 2) * (peers - 2 * half)
        return lax.rem(me + step, peers)

    loads = [
        pltpu.make_async_copy(src, dst, load_sem.at[i])
        for i, (src, dst) in enumerate((
            (x_hbm, x_own),
            (dy_hbm, dy_own),
            (down_hbm, down_ref),
            (up_hbm, up_ref),
            (wiring.at[ahead], counts),
            (wiring.at[section], tables.at[0]),
            (wiring.at[ahead], tables.at[1]),
            (dy_hbm.at[me], dy_got.at[me]),
        ))
    ]
    for copy in loads:
        copy.start()

    barrier = pltpu.get_barrier_semaphore()

    @pl.loop(0, peers)
    def _(t):
        who = turn(t)
        for where in (after, ahead):
            pl.semaphore_signal(
                barrier, inc=1, device_id={"section": where, "peer": who}, device_id_type=MESH
            )

    @pl.loop(1, peers)
    def _(t):
        pl.semaphore_signal(
            barrier, inc=1, device_id={"section": section, "peer": turn(t)}, device_id_type=MESH
        )

    pl.semaphore_wait(barrier, 3 * peers - 1)

    def remote(src, dst, sems, where, who):
        return pltpu.make_async_remote_copy(
            src_ref=src.at[who],
            dst_ref=dst.at[me],
            send_sem=sems.at[0, who],
            recv_sem=sems.at[1, me],
            device_id={"section": where, "peer": who},
            device_id_type=MESH,
        )

    def arrival(src, dst, sems, where, who):
        return pltpu.make_async_remote_copy(
            src_ref=src.at[who],
            dst_ref=dst.at[who],
            send_sem=sems.at[0, who],
            recv_sem=sems.at[1, who],
            device_id={"section": where, "peer": who},
            device_id_type=MESH,
        )

    @pl.loop(1, peers)
    def _(t):
        remote(dy_hbm, dy_got, dy1, section, turn(t)).start()

    for copy in loads:
        copy.wait()

    def cols(c):
        return pl.ds(pl.multiple_of(c * WIDE, WIDE), WIDE)

    def wide(ref, at):
        return ref[:, :, at].astype(F32).reshape(rows, WIDE)

    def tall(value):
        return value.reshape(blocks, blk, WIDE).astype(BF16)

    def inverse(x_ref):
        def squares(c, total):
            xc = wide(x_ref, cols(c))
            return total + jnp.sum(xc * xc, axis=1, keepdims=True)

        ms = lax.fori_loop(0, chunks, squares, jnp.zeros((rows, 1), F32)) / width
        return lax.rsqrt(ms + 1e-05)

    def project(x_ref, rinv, at):
        nc = (wide(x_ref, at) * rinv * g_ref[:, at]).astype(BF16)
        return nc, jnp.dot(nc, down_ref[at, :], preferred_element_type=F32)

    zero = jnp.zeros((rows, rank), F32)

    def head(x_ref, dy_ref):
        rinv = inverse(x_ref)

        def both(c, carry):
            pre, dact = carry
            at = cols(c)
            nc, part = project(x_ref, rinv, at)
            normed[:, at] = nc
            dact = dact + mul(wide(dy_ref, at).astype(BF16), up_ref[:, at], 1, 1)
            return pre + part, dact

        pre, dact = lax.fori_loop(0, chunks, both, (zero, zero))
        sig = jax.nn.sigmoid(pre)
        act = (pre * sig).astype(BF16)
        dpre = (dact * sig * (1.0 + pre * (1.0 - sig))).astype(BF16)
        return rinv, act, dpre

    def gradients(at, dy_ref, act, dpre, up_to, down_to):
        up_to[:, :, at] = tall(mul(act, wide(dy_ref, at).astype(BF16), 0, 0))
        down_to[at, :] = mul(normed[:, at], dpre, 0, 0).astype(BF16)

    rinv, act, dpre = head(x_own, dy_own)

    def tail(c, inner):
        at = cols(c)
        dn = mul(dpre, down_ref[at, :], 1, 1) * g_ref[:, at]
        dns[:, at] = dn
        return inner + jnp.sum(dn * wide(x_own, at), axis=1, keepdims=True)

    inner = lax.fori_loop(0, chunks, tail, jnp.zeros((rows, 1), F32)) / width
    pull = rinv * rinv * inner

    @pl.loop(0, chunks)
    def _(c):
        at = cols(c)
        dxs[:, :, at] = tall(wide(dy_own, at) + rinv * (dns[:, at] - wide(x_own, at) * pull))

    def spread(q, start):
        for slot in range(CAP):
            back[q, slot] = dxs[jnp.minimum(start + slot, blocks - 1)]
        return start + counts[q, me]

    lax.fori_loop(0, peers, spread, jnp.int32(0))

    @pl.loop(0, EARLY)
    def _(t):
        remote(back, back_out, sems_b, ahead, turn(t)).start()

    @pl.loop(0, chunks)
    def _(c):
        gradients(cols(c), dy_own, act, dpre, gup, gdown)

    saves = [
        pltpu.make_async_copy(gup, gup_out, out_sem.at[0]),
        pltpu.make_async_copy(gdown, gdown_out, out_sem.at[1]),
    ]
    for copy in saves:
        copy.start()

    mask = masks[section]
    graph, left, _ = colours(tables[0].astype(F32))
    graph_ref[...] = graph
    left_ref[...] = left

    def order(peer):
        return cut(
            left_ref[...], blocks, blk, lambda k: peer * peers + k, lambda b: peer * peers + b
        )

    mine = order(me)

    @pl.loop(0, chunks)
    def _(c):
        at = cols(c)
        x_pack[:, :, at] = tall(mul(mine, wide(x_own, at).astype(BF16)))

    x_got[me] = x_pack[me]

    @pl.loop(1, peers)
    def _(t):
        remote(x_pack, x_got, x1, section, turn(t)).start()

    @pl.loop(EARLY, peers)
    def _(t):
        remote(back, back_out, sems_b, ahead, turn(t)).start()

    @pl.loop(1, peers)
    def _(t):
        arrival(dy_hbm, dy_got, dy1, section, turn(t)).wait_recv()

    @pl.loop(0, peers)
    def _(p):
        dy_send[p] = dy_got[jnp.bitwise_xor(p, mask)]

    dy_pair[me] = dy_send[me]

    @pl.loop(1, peers)
    def _(t):
        remote(dy_send, dy_pair, dy2, section, turn(t)).start()

    _, _, right = colours(tables[1].astype(F32))
    e = right.shape[0]
    spots = iota((8, e), 1) - me * peers
    value = jnp.where((spots >= 0) & (spots < peers), spots, 0).astype(F32)
    found = mul(value.astype(BF16), right).astype(BF16)
    lanes = place_out.shape[1]
    near = hot(iota((e, lanes), 0) - me * peers == iota((e, lanes), 1))
    place_out[...] = (mul(found, near) + 0.5).astype(jnp.int32)

    @pl.loop(1, peers)
    def _(t):
        arrival(x_pack, x_got, x1, section, turn(t)).wait_recv()

    @pl.loop(0, peers)
    def _(p):
        x_send[p] = x_got[jnp.bitwise_xor(p, mask)]

    x_pair[me] = x_send[me]

    @pl.loop(1, peers)
    def _(t):
        remote(x_send, x_pair, x2, section, turn(t)).start()

    rinv_got = inverse(x_got)
    pre_got = lax.fori_loop(
        0, chunks, lambda c, pre: pre + project(x_got, rinv_got, cols(c))[1], zero
    )
    act_got = (pre_got * jax.nn.sigmoid(pre_got)).astype(BF16)
    sorting = cut(
        graph_ref[...], blocks, blk, lambda q: q * peers + me, lambda p: p * peers + me
    )

    @pl.loop(0, chunks)
    def _(c):
        at = cols(c)
        oc = (wide(x_got, at) + mul(act_got, up_ref[:, at])).astype(BF16)
        fwd[:, :, at] = tall(mul(sorting, oc))

    @pl.loop(0, peers)
    def _(t):
        remote(fwd, fwd_out, sems_f, after, turn(t)).start()

    theirs = order(jnp.bitwise_xor(me, mask))

    @pl.loop(1, peers)
    def _(t):
        who = turn(t)
        arrival(dy_send, dy_pair, dy2, section, who).wait_recv()
        arrival(x_send, x_pair, x2, section, who).wait_recv()

    @pl.loop(0, chunks)
    def _(c):
        at = cols(c)
        x_flat[:, :, at] = tall(mul(theirs, wide(x_pair, at).astype(BF16), 0, 0))

    _, act2, dpre2 = head(x_flat, dy_pair)

    @pl.loop(0, chunks)
    def _(c):
        gradients(cols(c), dy_pair, act2, dpre2, gup2, gdown2)

    saves += [
        pltpu.make_async_copy(gup2, gup2_out, out_sem.at[2]),
        pltpu.make_async_copy(gdown2, gdown2_out, out_sem.at[3]),
    ]
    for copy in saves[2:]:
        copy.start()

    @pl.loop(1, peers)
    def _(t):
        who = turn(t)
        remote(dy_hbm, dy_got, dy1, section, who).wait_send()
        remote(x_pack, x_got, x1, section, who).wait_send()
        remote(dy_send, dy_pair, dy2, section, who).wait_send()
        remote(x_send, x_pair, x2, section, who).wait_send()

    @pl.loop(0, peers)
    def _(t):
        who = turn(t)
        remote(fwd, fwd_out, sems_f, after, who).wait_send()
        remote(back, back_out, sems_b, ahead, who).wait_send()
        arrival(back, back_out, sems_b, ahead, who).wait_recv()
        arrival(fwd, fwd_out, sems_f, after, who).wait_recv()

    for copy in saves:
        copy.wait()


def run_section(masks, g, wiring, x, dy, down, up, sections, peers):
    vmem = pl.BlockSpec(memory_space=pltpu.VMEM)
    smem = pl.BlockSpec(memory_space=pltpu.SMEM)
    hbm = pl.BlockSpec(memory_space=pl.ANY)
    dma = pltpu.SemaphoreType.DMA
    blocks, blk, width = x.shape
    rows, rank = blocks * blk, up.shape[0]
    piece = pltpu.VMEM(x.shape, BF16)
    slots = (peers, CAP, blk, width)
    up3 = (peers, rank // peers, width)
    ups, downs = pltpu.VMEM(up3, BF16), pltpu.VMEM(down.shape, BF16)
    links = pltpu.VMEM((peers * blocks, peers * blocks), BF16)
    return pl.pallas_call(
        functools.partial(section_kernel, sections, peers),
        name="section_layer",
        in_specs=[smem, vmem] + [hbm] * 5,
        out_specs=[hbm] * 6 + [vmem],
        out_shape=[
            jax.ShapeDtypeStruct(x.shape, BF16),
            jax.ShapeDtypeStruct(slots, BF16),
            jax.ShapeDtypeStruct(up3, BF16),
            jax.ShapeDtypeStruct(down.shape, BF16),
            jax.ShapeDtypeStruct(up3, BF16),
            jax.ShapeDtypeStruct(down.shape, BF16),
            jax.ShapeDtypeStruct((8, 128), jnp.int32),
        ],
        scratch_shapes=[piece, piece, downs, pltpu.VMEM(up.shape, BF16)]
        + [piece] * 8
        + [
            pltpu.VMEM((rows, width), BF16), pltpu.VMEM((rows, width), F32),
            piece, piece, pltpu.VMEM(slots, BF16),
            ups, downs, ups, downs, links, links,
            pltpu.SMEM((peers, peers), jnp.int32),
            pltpu.VMEM((2, peers, peers), jnp.int32),
            dma((8,)), dma((2,)), dma((4,)),
        ]
        + [dma((2, peers))] * 6,
        compiler_params=pltpu.CompilerParams(
            collective_id=0, has_side_effects=True, vmem_limit_bytes=60 * 1024 * 1024
        ),
    )(masks, g, wiring, x, dy, down, up)


def settle_kernel(
    wiring, place, fwd, back, up, down, up2, down2,
    next_out, ret_out, gdown_out, gup_out,
    counts, places, nexts, rets, ups, downs, up2s, down2s, gups, gdowns,
    count_sem, row_sem, read_sem, write_sem,
):
    section = lax.axis_index("section")
    me = lax.axis_index("peer")
    tables = [
        pltpu.make_async_copy(wiring.at[section], counts, count_sem.at[0]),
        pltpu.make_async_copy(place, places, count_sem.at[1]),
    ]
    for copy in tables:
        copy.start()
    peers = counts.shape[0]

    def part(ref, c):
        size = ref.shape[0] // PARTS
        return ref.at[pl.ds(c * size, size)]

    pairs = ((up, ups), (up2, up2s), (down, downs), (down2, down2s))
    reads = [
        [
            pltpu.make_async_copy(part(src, c), part(dst, c), read_sem.at[c, i])
            for i, (src, dst) in enumerate(pairs)
        ]
        for c in range(PARTS)
    ]
    for copy in reads[0]:
        copy.start()
    for copy in tables:
        copy.wait()

    def gather(p, start):
        pltpu.make_async_copy(fwd.at[places[0, p]], nexts.at[p], row_sem.at[0, p]).start()
        n = counts[me, p]
        for slot in range(CAP):
            @pl.when(slot < n)
            def _():
                at = start + slot
                pltpu.make_async_copy(back.at[p, slot], rets.at[at], row_sem.at[1, at]).start()

        return start + n

    lax.fori_loop(0, peers, gather, jnp.int32(0))
    for group in reads[1:]:
        for copy in group:
            copy.start()

    writes = []
    for c in range(PARTS):
        for copy in reads[c]:
            copy.wait()
        for a, b, total, out, i in (
            (ups, up2s, gups, gup_out, 0),
            (downs, down2s, gdowns, gdown_out, 1),
        ):
            size = a.shape[0] // PARTS
            at = pl.ds(c * size, size)
            total[at] = (a[at].astype(F32) + b[at].astype(F32)) * 0.5
            writes.append(
                pltpu.make_async_copy(part(total, c), part(out, c), write_sem.at[c, i])
            )
            writes[-1].start()

    for k, (source, target, out) in enumerate(
        ((fwd.at[0], nexts, next_out), (back.at[0, 0], rets, ret_out))
    ):
        @pl.loop(0, peers)
        def _(b):
            pltpu.make_async_copy(source, target.at[b], row_sem.at[k, b]).wait()

        writes.append(pltpu.make_async_copy(target, out, write_sem.at[PARTS, k]))
        writes[-1].start()
    for copy in writes:
        copy.wait()


def settle(wiring, place, fwd, back, up, down, up2, down2):
    hbm = pl.BlockSpec(memory_space=pl.ANY)
    dma = pltpu.SemaphoreType.DMA
    peers, blk, width = fwd.shape
    rows = (peers, blk, width)
    return pl.pallas_call(
        settle_kernel,
        name="settle",
        in_specs=[hbm] * 8,
        out_specs=[hbm] * 4,
        out_shape=[
            jax.ShapeDtypeStruct(rows, BF16),
            jax.ShapeDtypeStruct(rows, BF16),
            jax.ShapeDtypeStruct(down.shape, F32),
            jax.ShapeDtypeStruct(up.shape, F32),
        ],
        scratch_shapes=[
            pltpu.SMEM((peers, peers), jnp.int32),
            pltpu.SMEM(place.shape, jnp.int32),
            pltpu.VMEM(rows, BF16), pltpu.VMEM(rows, BF16),
            pltpu.VMEM(up.shape, BF16), pltpu.VMEM(down.shape, BF16),
            pltpu.VMEM(up.shape, BF16), pltpu.VMEM(down.shape, BF16),
            pltpu.VMEM(up.shape, F32), pltpu.VMEM(down.shape, F32),
            dma((2,)), dma((2, peers)), dma((PARTS, 4)), dma((PARTS + 1, 2)),
        ],
    )(wiring, place, fwd, back, up, down, up2, down2)


def body(inputs, out_grad, gains, down_proj, up_proj, wiring, pair_mask):
    sections = lax.axis_size("section")
    peers = lax.axis_size("peer")
    rows, width = inputs.shape[2:]
    rank = down_proj.shape[2]
    pieces = (peers, rows // peers, width)
    fwd, back, up, down, up2, down2, place = run_section(
        pair_mask, gains, wiring, inputs.reshape(pieces), out_grad.reshape(pieces),
        down_proj[0], up_proj[0], sections, peers,
    )
    next_rows, return_rows, grad_down, grad_up = settle(
        wiring, place, fwd, back, up, down, up2, down2
    )
    return (
        next_rows.reshape(1, 1, rows, width),
        return_rows.reshape(1, 1, rows, width),
        grad_down.reshape(1, 1, width, rank),
        grad_up.reshape(1, 1, rank, width),
    )


def solution(mesh):
    placed = (
        P("section", "peer", None, None),
        P("section", "peer", None, None),
        P("section", None),
        P("section", None, None),
        P("section", None, None),
        P(),
        P(),
    )
    return jax.shard_map(
        body,
        mesh=mesh,
        in_specs=placed,
        out_specs=(
            P("section", "peer", None, None),
            P("section", "peer", None, None),
            P("section", "peer", None, None),
            P("section", "peer", None, None),
        ),
        check_vma=False,
    )
```

```python
import functools

import jax
import jax.numpy as jnp
from jax import lax
from jax.experimental import pallas as pl
from jax.experimental.pallas import tpu as pltpu
from jax.sharding import PartitionSpec as P

CAP = 2
WIDE = 512
EARLY = 8
MESH = pl.DeviceIdType.MESH
F32, BF16 = jnp.float32, jnp.bfloat16


def dims(a, b):
    return (((a,), (b,)), ((), ()))


def mul(a, b, ca=1, cb=0):
    return lax.dot_general(a, b, dims(ca, cb), preferred_element_type=F32)


def hot(mask):
    return mask.astype(F32).astype(BF16)


def iota(shape, dim):
    return lax.broadcasted_iota(jnp.int32, shape, dim)


def block_graph(counts):
    n = counts.shape[0]
    e, bits = n * n, n.bit_length() - 1
    c = counts.astype(BF16)
    start = mul(c, hot(iota((n, n), 0) < iota((n, n), 1)))
    above = mul(hot(iota((n, n), 1) < iota((n, n), 0)), c)
    right = hot((iota((e, n), 0) >> bits) == iota((e, n), 1))
    left = hot((iota((n, e), 1) >> bits) == iota((n, e), 0))

    def grow(m):
        return mul(mul(right, m.astype(BF16), 1, 1).astype(BF16), left)

    rank = (iota((e, e), 1) & (n - 1)).astype(F32) - grow(start)
    place = (iota((e, e), 0) & (n - 1)).astype(F32)
    inside = (rank >= 0) & (rank < grow(counts)) & (place == grow(above) + rank)
    return hot(inside)


def halve(graph, left, right, size):
    e = graph.shape[0]
    row, col = iota((e, e), 0), iota((e, e), 1)
    swap = hot((row >> 1 == col >> 1) & (row != col))
    mate = mul(graph, mul(swap, graph).astype(BF16), 0, 0).astype(BF16)
    step = mul(mate, swap).astype(BF16)

    def jump(_, carry):
        low, step = carry
        low = jnp.minimum(low, mul(low.astype(BF16), step))
        return low, mul(step, step).astype(BF16)

    longest = e * size >> (e.bit_length() - 1) // 2 + 1
    low, _ = lax.fori_loop(0, longest.bit_length() - 1, jump, (iota((8, e), 1).astype(F32), step))
    side = (low > mul(low.astype(BF16), swap)).astype(F32)
    at = iota((8, e), 1)
    base = ((at & ~(size - 1)) + ((at & (size - 1)) >> 1)).astype(F32)

    def moved(half):
        return hot(row.astype(F32) == (base + half * (size // 2))[0:1, :])

    on_left, on_right = moved(side), moved(mul(side.astype(BF16), graph, 1, 1))
    graph = mul(mul(on_right, graph).astype(BF16), on_left, 1, 1).astype(BF16)
    return graph, mul(on_left, left).astype(BF16), mul(on_right, right).astype(BF16)


def colours(counts):
    graph = block_graph(counts)
    size, e = counts.shape[0], graph.shape[0]
    left = right = hot(iota((e, e), 0) == iota((e, e), 1))
    while size > 1:
        graph, left, right = halve(graph, left, right, size)
        size //= 2
    return graph, left, right


def cut(matrix, blocks, blk, rows_at, cols_at):
    e, n, bits = matrix.shape[0], blocks * blk, blk.bit_length() - 1
    pick = hot(iota((n, e), 1) == rows_at(iota((n, e), 0) >> bits))
    take = hot(iota((e, n), 0) == cols_at(iota((e, n), 1) >> bits))
    found = mul(mul(pick, matrix).astype(BF16), take)
    same = (iota((n, n), 0) & (blk - 1)) == (iota((n, n), 1) & (blk - 1))
    return hot(same & (found > 0.5))


def section_kernel(
    sections, peers, masks, g_ref, wiring, x_hbm, dy_hbm, down_hbm, up_hbm,
    fwd_out, back_out, gup_out, gdown_out, place_out,
    x_own, dy_own, down_ref, up_ref, x_pack, x_got, dy_got, x_send, dy_send, x_pair, dy_pair,
    x_flat, normed, dns, dxs, fwd, back, gup, gdown, graph_ref, left_ref,
    counts, tables, load_sem, x1, dy1, x2, dy2, sems_f, sems_b,
):
    section = lax.axis_index("section")
    me = lax.axis_index("peer")
    after = lax.rem(section + 1, sections)
    ahead = lax.rem(section + sections - 1, sections)
    blocks, blk, width = x_own.shape
    rows = blocks * blk
    rank = up_ref.shape[0]
    chunks = width // WIDE

    def turn(t):
        half = (t + 1) // 2
        step = half + (1 - t % 2) * (peers - 2 * half)
        return lax.rem(me + step, peers)

    loads = [
        pltpu.make_async_copy(src, dst, load_sem.at[i])
        for i, (src, dst) in enumerate((
            (x_hbm, x_own),
            (dy_hbm, dy_own),
            (down_hbm, down_ref),
            (up_hbm, up_ref),
            (wiring.at[ahead], counts),
            (wiring.at[section], tables.at[0]),
            (wiring.at[ahead], tables.at[1]),
            (dy_hbm.at[me], dy_got.at[me]),
        ))
    ]
    for copy in loads:
        copy.start()

    barrier = pltpu.get_barrier_semaphore()

    @pl.loop(0, peers)
    def _(t):
        who = turn(t)
        for where in (after, ahead):
            pl.semaphore_signal(
                barrier, inc=1, device_id={"section": where, "peer": who}, device_id_type=MESH
            )

    @pl.loop(1, peers)
    def _(t):
        pl.semaphore_signal(
            barrier, inc=1, device_id={"section": section, "peer": turn(t)}, device_id_type=MESH
        )

    pl.semaphore_wait(barrier, 3 * peers - 1)

    def remote(src, dst, sems, where, who):
        return pltpu.make_async_remote_copy(
            src_ref=src.at[who],
            dst_ref=dst.at[me],
            send_sem=sems.at[0, who],
            recv_sem=sems.at[1, me],
            device_id={"section": where, "peer": who},
            device_id_type=MESH,
        )

    def arrival(src, dst, sems, where, who):
        return pltpu.make_async_remote_copy(
            src_ref=src.at[who],
            dst_ref=dst.at[who],
            send_sem=sems.at[0, who],
            recv_sem=sems.at[1, who],
            device_id={"section": where, "peer": who},
            device_id_type=MESH,
        )

    @pl.loop(1, peers)
    def _(t):
        remote(dy_hbm, dy_got, dy1, section, turn(t)).start()

    for copy in loads:
        copy.wait()

    def cols(c):
        return pl.ds(pl.multiple_of(c * WIDE, WIDE), WIDE)

    def wide(ref, at):
        return ref[:, :, at].astype(F32).reshape(rows, WIDE)

    def tall(value):
        return value.reshape(blocks, blk, WIDE).astype(BF16)

    def inverse(x_ref):
        def squares(c, total):
            xc = wide(x_ref, cols(c))
            return total + jnp.sum(xc * xc, axis=1, keepdims=True)

        ms = lax.fori_loop(0, chunks, squares, jnp.zeros((rows, 1), F32)) / width
        return lax.rsqrt(ms + 1e-05)

    def project(x_ref, rinv, at):
        nc = (wide(x_ref, at) * rinv * g_ref[:, at]).astype(BF16)
        return nc, jnp.dot(nc, down_ref[at, :], preferred_element_type=F32)

    zero = jnp.zeros((rows, rank), F32)

    def head(x_ref, dy_ref):
        rinv = inverse(x_ref)

        def both(c, carry):
            pre, dact = carry
            at = cols(c)
            nc, part = project(x_ref, rinv, at)
            normed[:, at] = nc
            dact = dact + mul(wide(dy_ref, at).astype(BF16), up_ref[:, at], 1, 1)
            return pre + part, dact

        pre, dact = lax.fori_loop(0, chunks, both, (zero, zero))
        sig = jax.nn.sigmoid(pre)
        act = (pre * sig).astype(BF16)
        dpre = (dact * sig * (1.0 + pre * (1.0 - sig))).astype(BF16)
        return rinv, act, dpre

    def gradients(at, dy_ref, act, dpre):
        up_part = tall(mul(act, wide(dy_ref, at).astype(BF16), 0, 0))
        return up_part, mul(normed[:, at], dpre, 0, 0).astype(BF16)

    rinv, act, dpre = head(x_own, dy_own)

    def tail(c, inner):
        at = cols(c)
        dn = mul(dpre, down_ref[at, :], 1, 1) * g_ref[:, at]
        dns[:, at] = dn
        return inner + jnp.sum(dn * wide(x_own, at), axis=1, keepdims=True)

    inner = lax.fori_loop(0, chunks, tail, jnp.zeros((rows, 1), F32)) / width
    pull = rinv * rinv * inner

    @pl.loop(0, chunks)
    def _(c):
        at = cols(c)
        dxs[:, :, at] = tall(wide(dy_own, at) + rinv * (dns[:, at] - wide(x_own, at) * pull))

    def spread(q, start):
        for slot in range(CAP):
            back[q, slot] = dxs[jnp.minimum(start + slot, blocks - 1)]
        return start + counts[q, me]

    lax.fori_loop(0, peers, spread, jnp.int32(0))

    @pl.loop(0, EARLY)
    def _(t):
        remote(back, back_out, sems_b, ahead, turn(t)).start()

    @pl.loop(0, chunks)
    def _(c):
        at = cols(c)
        gup[:, :, at], gdown[at, :] = gradients(at, dy_own, act, dpre)

    mask = masks[section]
    graph, left, _ = colours(tables[0].astype(F32))
    graph_ref[...] = graph
    left_ref[...] = left

    def order(peer):
        return cut(
            left_ref[...], blocks, blk, lambda k: peer * peers + k, lambda b: peer * peers + b
        )

    mine = order(me)

    @pl.loop(0, chunks)
    def _(c):
        at = cols(c)
        x_pack[:, :, at] = tall(mul(mine, wide(x_own, at).astype(BF16)))

    x_got[me] = x_pack[me]

    @pl.loop(1, peers)
    def _(t):
        remote(x_pack, x_got, x1, section, turn(t)).start()

    @pl.loop(EARLY, peers)
    def _(t):
        remote(back, back_out, sems_b, ahead, turn(t)).start()

    @pl.loop(1, peers)
    def _(t):
        arrival(dy_hbm, dy_got, dy1, section, turn(t)).wait_recv()

    @pl.loop(0, peers)
    def _(p):
        dy_send[p] = dy_got[jnp.bitwise_xor(p, mask)]

    dy_pair[me] = dy_send[me]

    @pl.loop(1, peers)
    def _(t):
        remote(dy_send, dy_pair, dy2, section, turn(t)).start()

    _, _, right = colours(tables[1].astype(F32))
    e = right.shape[0]
    spots = iota((8, e), 1) - me * peers
    value = jnp.where((spots >= 0) & (spots < peers), spots, 0).astype(F32)
    found = mul(value.astype(BF16), right).astype(BF16)
    lanes = place_out.shape[1]
    near = hot(iota((e, lanes), 0) - me * peers == iota((e, lanes), 1))
    place_out[...] = (mul(found, near) + 0.5).astype(jnp.int32)

    @pl.loop(1, peers)
    def _(t):
        arrival(x_pack, x_got, x1, section, turn(t)).wait_recv()

    @pl.loop(0, peers)
    def _(p):
        x_send[p] = x_got[jnp.bitwise_xor(p, mask)]

    x_pair[me] = x_send[me]

    @pl.loop(1, peers)
    def _(t):
        remote(x_send, x_pair, x2, section, turn(t)).start()

    rinv_got = inverse(x_got)
    pre_got = lax.fori_loop(
        0, chunks, lambda c, pre: pre + project(x_got, rinv_got, cols(c))[1], zero
    )
    act_got = (pre_got * jax.nn.sigmoid(pre_got)).astype(BF16)
    sorting = cut(
        graph_ref[...], blocks, blk, lambda q: q * peers + me, lambda p: p * peers + me
    )

    @pl.loop(0, chunks)
    def _(c):
        at = cols(c)
        oc = (wide(x_got, at) + mul(act_got, up_ref[:, at])).astype(BF16)
        fwd[:, :, at] = tall(mul(sorting, oc))

    @pl.loop(0, peers)
    def _(t):
        remote(fwd, fwd_out, sems_f, after, turn(t)).start()

    theirs = order(jnp.bitwise_xor(me, mask))

    @pl.loop(1, peers)
    def _(t):
        who = turn(t)
        arrival(dy_send, dy_pair, dy2, section, who).wait_recv()
        arrival(x_send, x_pair, x2, section, who).wait_recv()

    @pl.loop(0, chunks)
    def _(c):
        at = cols(c)
        x_flat[:, :, at] = tall(mul(theirs, wide(x_pair, at).astype(BF16), 0, 0))

    _, act2, dpre2 = head(x_flat, dy_pair)

    @pl.loop(0, chunks)
    def _(c):
        at = cols(c)
        up_part, down_part = gradients(at, dy_pair, act2, dpre2)
        gup_out[:, :, at] = (gup[:, :, at].astype(F32) + up_part.astype(F32)) * 0.5
        gdown_out[at, :] = (gdown[at, :].astype(F32) + down_part.astype(F32)) * 0.5

    @pl.loop(1, peers)
    def _(t):
        who = turn(t)
        remote(dy_hbm, dy_got, dy1, section, who).wait_send()
        remote(x_pack, x_got, x1, section, who).wait_send()
        remote(dy_send, dy_pair, dy2, section, who).wait_send()
        remote(x_send, x_pair, x2, section, who).wait_send()

    @pl.loop(0, peers)
    def _(t):
        who = turn(t)
        remote(fwd, fwd_out, sems_f, after, who).wait_send()
        remote(back, back_out, sems_b, ahead, who).wait_send()
        arrival(back, back_out, sems_b, ahead, who).wait_recv()
        arrival(fwd, fwd_out, sems_f, after, who).wait_recv()


def run_section(masks, g, wiring, x, dy, down, up, sections, peers):
    vmem = pl.BlockSpec(memory_space=pltpu.VMEM)
    smem = pl.BlockSpec(memory_space=pltpu.SMEM)
    hbm = pl.BlockSpec(memory_space=pl.ANY)
    dma = pltpu.SemaphoreType.DMA
    blocks, blk, width = x.shape
    rows, rank = blocks * blk, up.shape[0]
    piece = pltpu.VMEM(x.shape, BF16)
    slots = (peers, CAP, blk, width)
    up3 = (peers, rank // peers, width)
    ups, downs = pltpu.VMEM(up3, BF16), pltpu.VMEM(down.shape, BF16)
    links = pltpu.VMEM((peers * blocks, peers * blocks), BF16)
    return pl.pallas_call(
        functools.partial(section_kernel, sections, peers),
        name="section_layer",
        in_specs=[smem, vmem] + [hbm] * 5,
        out_specs=[vmem] * 5,
        out_shape=[
            pltpu.VMEM(x.shape, BF16),
            pltpu.VMEM(slots, BF16),
            pltpu.VMEM(up3, F32),
            pltpu.VMEM(down.shape, F32),
            pltpu.VMEM((8, 128), jnp.int32),
        ],
        scratch_shapes=[piece, piece, downs, pltpu.VMEM(up.shape, BF16)]
        + [piece] * 8
        + [
            pltpu.VMEM((rows, width), BF16), pltpu.VMEM((rows, width), F32),
            piece, piece, pltpu.VMEM(slots, BF16),
            ups, downs, links, links,
            pltpu.SMEM((peers, peers), jnp.int32),
            pltpu.VMEM((2, peers, peers), jnp.int32),
            dma((8,)),
        ]
        + [dma((2, peers))] * 6,
        compiler_params=pltpu.CompilerParams(
            collective_id=0, has_side_effects=True, vmem_limit_bytes=48 * 1024 * 1024
        ),
    )(masks, g, wiring, x, dy, down, up)


def settle_kernel(
    wiring, place, fwd, back, up, down, next_out, ret_out, gdown_out, gup_out,
    counts, places, count_sem, row_sem, sum_sem,
):
    me = lax.axis_index("peer")
    peers = counts.shape[0]
    tables = [
        pltpu.make_async_copy(wiring.at[lax.axis_index("section")], counts, count_sem.at[0]),
        pltpu.make_async_copy(place, places, count_sem.at[1]),
    ]
    sums = [
        pltpu.make_async_copy(up, gup_out, sum_sem.at[0]),
        pltpu.make_async_copy(down, gdown_out, sum_sem.at[1]),
    ]
    for copy in tables + sums:
        copy.start()
    for copy in tables:
        copy.wait()

    def gather(p, start):
        pltpu.make_async_copy(fwd.at[places[0, p]], next_out.at[p], row_sem.at[0, p]).start()
        n = counts[me, p]
        for slot in range(CAP):
            @pl.when(slot < n)
            def _():
                at = start + slot
                pltpu.make_async_copy(back.at[p, slot], ret_out.at[at], row_sem.at[1, at]).start()

        return start + n

    lax.fori_loop(0, peers, gather, jnp.int32(0))

    @pl.loop(0, peers)
    def _(p):
        pltpu.make_async_copy(fwd.at[p], next_out.at[p], row_sem.at[0, p]).wait()
        pltpu.make_async_copy(back.at[p, 0], ret_out.at[p], row_sem.at[1, p]).wait()

    for copy in sums:
        copy.wait()


def settle(wiring, place, fwd, back, up, down):
    hbm = pl.BlockSpec(memory_space=pl.ANY)
    vmem = pl.BlockSpec(memory_space=pltpu.VMEM)
    dma = pltpu.SemaphoreType.DMA
    peers = fwd.shape[0]
    return pl.pallas_call(
        settle_kernel,
        name="settle",
        in_specs=[hbm] + [vmem] * 5,
        out_specs=[hbm] * 4,
        out_shape=[
            jax.ShapeDtypeStruct(fwd.shape, BF16),
            jax.ShapeDtypeStruct(fwd.shape, BF16),
            jax.ShapeDtypeStruct(down.shape, F32),
            jax.ShapeDtypeStruct(up.shape, F32),
        ],
        scratch_shapes=[
            pltpu.SMEM((peers, peers), jnp.int32),
            pltpu.SMEM(place.shape, jnp.int32),
            dma((2,)), dma((2, peers)), dma((2,)),
        ],
        compiler_params=pltpu.CompilerParams(vmem_limit_bytes=16 * 1024 * 1024),
    )(wiring, *(pltpu.with_memory_space_constraint(a, pltpu.VMEM) for a in (place, fwd, back, up, down)))


def body(inputs, out_grad, gains, down_proj, up_proj, wiring, pair_mask):
    sections = lax.axis_size("section")
    peers = lax.axis_size("peer")
    rows, width = inputs.shape[2:]
    rank = down_proj.shape[2]
    pieces = (peers, rows // peers, width)
    fwd, back, up, down, place = run_section(
        pair_mask, gains, wiring, inputs.reshape(pieces), out_grad.reshape(pieces),
        down_proj[0], up_proj[0], sections, peers,
    )
    next_rows, return_rows, grad_down, grad_up = settle(wiring, place, fwd, back, up, down)
    return (
        next_rows.reshape(1, 1, rows, width),
        return_rows.reshape(1, 1, rows, width),
        grad_down.reshape(1, 1, width, rank),
        grad_up.reshape(1, 1, rank, width),
    )


def solution(mesh):
    placed = (
        P("section", "peer", None, None),
        P("section", "peer", None, None),
        P("section", None),
        P("section", None, None),
        P("section", None, None),
        P(),
        P(),
    )
    return jax.shard_map(
        body,
        mesh=mesh,
        in_specs=placed,
        out_specs=(
            P("section", "peer", None, None),
            P("section", "peer", None, None),
            P("section", "peer", None, None),
            P("section", "peer", None, None),
        ),
        check_vma=False,
    )
```

```python
import functools

import jax
import jax.numpy as jnp
from jax import lax
from jax.experimental import pallas as pl
from jax.experimental.pallas import tpu as pltpu
from jax.sharding import PartitionSpec as P

CAP = 2
WIDE = 512
EARLY = 8
MESH = pl.DeviceIdType.MESH
F32, BF16 = jnp.float32, jnp.bfloat16


def dims(a, b):
    return (((a,), (b,)), ((), ()))


def mul(a, b, ca=1, cb=0):
    return lax.dot_general(a, b, dims(ca, cb), preferred_element_type=F32)


def hot(mask):
    return mask.astype(F32).astype(BF16)


def iota(shape, dim):
    return lax.broadcasted_iota(jnp.int32, shape, dim)


def block_graph(counts):
    n = counts.shape[0]
    e, bits = n * n, n.bit_length() - 1
    c = counts.astype(BF16)
    start = mul(c, hot(iota((n, n), 0) < iota((n, n), 1)))
    above = mul(hot(iota((n, n), 1) < iota((n, n), 0)), c)
    right = hot((iota((e, n), 0) >> bits) == iota((e, n), 1))
    left = hot((iota((n, e), 1) >> bits) == iota((n, e), 0))

    def grow(m):
        return mul(mul(right, m.astype(BF16), 1, 1).astype(BF16), left)

    rank = (iota((e, e), 1) & (n - 1)).astype(F32) - grow(start)
    place = (iota((e, e), 0) & (n - 1)).astype(F32)
    inside = (rank >= 0) & (rank < grow(counts)) & (place == grow(above) + rank)
    return hot(inside)


def halve(graph, left, right, size):
    e = graph.shape[0]
    row, col = iota((e, e), 0), iota((e, e), 1)
    swap = hot((row >> 1 == col >> 1) & (row != col))
    mate = mul(graph, mul(swap, graph).astype(BF16), 0, 0).astype(BF16)
    step = mul(mate, swap).astype(BF16)

    def jump(_, carry):
        low, step = carry
        low = jnp.minimum(low, mul(low.astype(BF16), step))
        return low, mul(step, step).astype(BF16)

    longest = e * size >> (e.bit_length() - 1) // 2 + 1
    low, _ = lax.fori_loop(0, longest.bit_length() - 1, jump, (iota((8, e), 1).astype(F32), step))
    side = (low > mul(low.astype(BF16), swap)).astype(F32)
    at = iota((8, e), 1)
    base = ((at & ~(size - 1)) + ((at & (size - 1)) >> 1)).astype(F32)

    def moved(half):
        return hot(row.astype(F32) == (base + half * (size // 2))[0:1, :])

    on_left, on_right = moved(side), moved(mul(side.astype(BF16), graph, 1, 1))
    graph = mul(mul(on_right, graph).astype(BF16), on_left, 1, 1).astype(BF16)
    return graph, mul(on_left, left).astype(BF16), mul(on_right, right).astype(BF16)


def colours(counts):
    graph = block_graph(counts)
    size, e = counts.shape[0], graph.shape[0]
    left = right = hot(iota((e, e), 0) == iota((e, e), 1))
    while size > 1:
        graph, left, right = halve(graph, left, right, size)
        size //= 2
    return graph, left, right


def cut(matrix, blocks, blk, rows_at, cols_at):
    e, n, bits = matrix.shape[0], blocks * blk, blk.bit_length() - 1
    pick = hot(iota((n, e), 1) == rows_at(iota((n, e), 0) >> bits))
    take = hot(iota((e, n), 0) == cols_at(iota((e, n), 1) >> bits))
    found = mul(mul(pick, matrix).astype(BF16), take)
    same = (iota((n, n), 0) & (blk - 1)) == (iota((n, n), 1) & (blk - 1))
    return hot(same & (found > 0.5))


def section_kernel(
    sections, peers, masks, g_ref, wiring, x_hbm, dy_hbm, down_hbm, up_hbm,
    fwd_out, back_out, gup_out, gdown_out, place_out,
    x_own, dy_own, down_ref, up_ref, x_pack, x_got, dy_got, x_send, dy_send, x_pair, dy_pair,
    x_flat, normed, dns, dxs, fwd, back, gup, gdown, graph_ref, left_ref,
    counts, tables, near, load_sem, x1, dy1, x2, dy2, sems_f, sems_b,
):
    section = lax.axis_index("section")
    me = lax.axis_index("peer")
    after = lax.rem(section + 1, sections)
    ahead = lax.rem(section + sections - 1, sections)
    blocks, blk, width = x_own.shape
    rows = blocks * blk
    rank = up_ref.shape[0]
    chunks = width // WIDE

    def turn(t):
        half = (t + 1) // 2
        step = half + (1 - t % 2) * (peers - 2 * half)
        return lax.rem(me + step, peers)

    loads = [
        pltpu.make_async_copy(src, dst, load_sem.at[i])
        for i, (src, dst) in enumerate((
            (x_hbm, x_own),
            (dy_hbm, dy_own),
            (down_hbm, down_ref),
            (up_hbm, up_ref),
            (wiring.at[ahead], counts),
            (wiring.at[section], tables.at[0]),
            (wiring.at[ahead], tables.at[1]),
            (dy_hbm.at[me], dy_got.at[me]),
        ))
    ]
    for copy in loads:
        copy.start()

    barrier = pltpu.get_barrier_semaphore()

    for where in (after, ahead):
        pl.semaphore_signal(
            barrier, inc=1, device_id={"section": where, "peer": me}, device_id_type=MESH
        )

    def greet(semaphore):
        @pl.loop(1, peers)
        def _(t):
            pl.semaphore_signal(
                semaphore, inc=1, device_id={"section": section, "peer": turn(t)}, device_id_type=MESH
            )

    greet(barrier)
    pl.semaphore_wait(barrier, peers + 1)

    def remote(src, dst, sems, where, who):
        return pltpu.make_async_remote_copy(
            src_ref=src.at[who],
            dst_ref=dst.at[me],
            send_sem=sems.at[0, who],
            recv_sem=sems.at[1, me],
            device_id={"section": where, "peer": who},
            device_id_type=MESH,
        )

    def arrival(src, dst, sems, where, who):
        return pltpu.make_async_remote_copy(
            src_ref=src.at[who],
            dst_ref=dst.at[who],
            send_sem=sems.at[0, who],
            recv_sem=sems.at[1, who],
            device_id={"section": where, "peer": who},
            device_id_type=MESH,
        )

    @pl.loop(1, peers)
    def _(t):
        remote(dy_hbm, dy_got, dy1, section, turn(t)).start()

    greet(near)

    for copy in loads:
        copy.wait()

    def cols(c):
        return pl.ds(pl.multiple_of(c * WIDE, WIDE), WIDE)

    def wide(ref, at):
        return ref[:, :, at].astype(F32).reshape(rows, WIDE)

    def tall(value):
        return value.reshape(blocks, blk, WIDE).astype(BF16)

    def inverse(x_ref):
        def squares(c, total):
            xc = wide(x_ref, cols(c))
            return total + jnp.sum(xc * xc, axis=1, keepdims=True)

        ms = lax.fori_loop(0, chunks, squares, jnp.zeros((rows, 1), F32)) / width
        return lax.rsqrt(ms + 1e-05)

    def project(x_ref, rinv, at):
        nc = (wide(x_ref, at) * rinv * g_ref[:, at]).astype(BF16)
        return nc, jnp.dot(nc, down_ref[at, :], preferred_element_type=F32)

    zero = jnp.zeros((rows, rank), F32)

    def head(x_ref, dy_ref):
        rinv = inverse(x_ref)

        def both(c, carry):
            pre, dact = carry
            at = cols(c)
            nc, part = project(x_ref, rinv, at)
            normed[:, at] = nc
            dact = dact + mul(wide(dy_ref, at).astype(BF16), up_ref[:, at], 1, 1)
            return pre + part, dact

        pre, dact = lax.fori_loop(0, chunks, both, (zero, zero))
        sig = jax.nn.sigmoid(pre)
        act = (pre * sig).astype(BF16)
        dpre = (dact * sig * (1.0 + pre * (1.0 - sig))).astype(BF16)
        return rinv, act, dpre

    def gradients(at, dy_ref, act, dpre):
        up_part = tall(mul(act, wide(dy_ref, at).astype(BF16), 0, 0))
        return up_part, mul(normed[:, at], dpre, 0, 0).astype(BF16)

    rinv, act, dpre = head(x_own, dy_own)

    def tail(c, inner):
        at = cols(c)
        dn = mul(dpre, down_ref[at, :], 1, 1) * g_ref[:, at]
        dns[:, at] = dn
        return inner + jnp.sum(dn * wide(x_own, at), axis=1, keepdims=True)

    inner = lax.fori_loop(0, chunks, tail, jnp.zeros((rows, 1), F32)) / width
    pull = rinv * rinv * inner

    @pl.loop(0, chunks)
    def _(c):
        at = cols(c)
        dxs[:, :, at] = tall(wide(dy_own, at) + rinv * (dns[:, at] - wide(x_own, at) * pull))

    def spread(q, start):
        for slot in range(CAP):
            back[q, slot] = dxs[jnp.minimum(start + slot, blocks - 1)]
        return start + counts[q, me]

    lax.fori_loop(0, peers, spread, jnp.int32(0))
    pl.semaphore_wait(near, peers - 1)

    @pl.loop(0, EARLY)
    def _(t):
        remote(back, back_out, sems_b, ahead, turn(t)).start()

    @pl.loop(0, chunks)
    def _(c):
        at = cols(c)
        gup[:, :, at], gdown[at, :] = gradients(at, dy_own, act, dpre)

    mask = masks[section]
    graph, left, _ = colours(tables[0].astype(F32))
    graph_ref[...] = graph
    left_ref[...] = left

    def order(peer):
        return cut(
            left_ref[...], blocks, blk, lambda k: peer * peers + k, lambda b: peer * peers + b
        )

    mine = order(me)

    @pl.loop(0, chunks)
    def _(c):
        at = cols(c)
        x_pack[:, :, at] = tall(mul(mine, wide(x_own, at).astype(BF16)))

    x_got[me] = x_pack[me]

    @pl.loop(1, peers)
    def _(t):
        remote(x_pack, x_got, x1, section, turn(t)).start()

    @pl.loop(EARLY, peers)
    def _(t):
        remote(back, back_out, sems_b, ahead, turn(t)).start()

    @pl.loop(1, peers)
    def _(t):
        arrival(dy_hbm, dy_got, dy1, section, turn(t)).wait_recv()

    @pl.loop(0, peers)
    def _(p):
        dy_send[p] = dy_got[jnp.bitwise_xor(p, mask)]

    dy_pair[me] = dy_send[me]

    @pl.loop(1, peers)
    def _(t):
        remote(dy_send, dy_pair, dy2, section, turn(t)).start()

    _, _, right = colours(tables[1].astype(F32))
    e = right.shape[0]
    spots = iota((8, e), 1) - me * peers
    value = jnp.where((spots >= 0) & (spots < peers), spots, 0).astype(F32)
    found = mul(value.astype(BF16), right).astype(BF16)
    lanes = place_out.shape[1]
    near = hot(iota((e, lanes), 0) - me * peers == iota((e, lanes), 1))
    place_out[...] = (mul(found, near) + 0.5).astype(jnp.int32)

    @pl.loop(1, peers)
    def _(t):
        arrival(x_pack, x_got, x1, section, turn(t)).wait_recv()

    @pl.loop(0, peers)
    def _(p):
        x_send[p] = x_got[jnp.bitwise_xor(p, mask)]

    x_pair[me] = x_send[me]

    @pl.loop(1, peers)
    def _(t):
        remote(x_send, x_pair, x2, section, turn(t)).start()

    rinv_got = inverse(x_got)
    pre_got = lax.fori_loop(
        0, chunks, lambda c, pre: pre + project(x_got, rinv_got, cols(c))[1], zero
    )
    act_got = (pre_got * jax.nn.sigmoid(pre_got)).astype(BF16)
    sorting = cut(
        graph_ref[...], blocks, blk, lambda q: q * peers + me, lambda p: p * peers + me
    )

    @pl.loop(0, chunks)
    def _(c):
        at = cols(c)
        oc = (wide(x_got, at) + mul(act_got, up_ref[:, at])).astype(BF16)
        fwd[:, :, at] = tall(mul(sorting, oc))

    @pl.loop(0, peers)
    def _(t):
        remote(fwd, fwd_out, sems_f, after, turn(t)).start()

    theirs = order(jnp.bitwise_xor(me, mask))

    @pl.loop(1, peers)
    def _(t):
        who = turn(t)
        arrival(dy_send, dy_pair, dy2, section, who).wait_recv()
        arrival(x_send, x_pair, x2, section, who).wait_recv()

    @pl.loop(0, chunks)
    def _(c):
        at = cols(c)
        x_flat[:, :, at] = tall(mul(theirs, wide(x_pair, at).astype(BF16), 0, 0))

    _, act2, dpre2 = head(x_flat, dy_pair)

    @pl.loop(0, chunks)
    def _(c):
        at = cols(c)
        up_part, down_part = gradients(at, dy_pair, act2, dpre2)
        gup_out[:, :, at] = (gup[:, :, at].astype(F32) + up_part.astype(F32)) * 0.5
        gdown_out[at, :] = (gdown[at, :].astype(F32) + down_part.astype(F32)) * 0.5

    @pl.loop(1, peers)
    def _(t):
        who = turn(t)
        remote(dy_hbm, dy_got, dy1, section, who).wait_send()
        remote(x_pack, x_got, x1, section, who).wait_send()
        remote(dy_send, dy_pair, dy2, section, who).wait_send()
        remote(x_send, x_pair, x2, section, who).wait_send()

    @pl.loop(0, peers)
    def _(t):
        who = turn(t)
        remote(fwd, fwd_out, sems_f, after, who).wait_send()
        remote(back, back_out, sems_b, ahead, who).wait_send()
        arrival(back, back_out, sems_b, ahead, who).wait_recv()
        arrival(fwd, fwd_out, sems_f, after, who).wait_recv()


def run_section(masks, g, wiring, x, dy, down, up, sections, peers):
    vmem = pl.BlockSpec(memory_space=pltpu.VMEM)
    smem = pl.BlockSpec(memory_space=pltpu.SMEM)
    hbm = pl.BlockSpec(memory_space=pl.ANY)
    dma = pltpu.SemaphoreType.DMA
    blocks, blk, width = x.shape
    rows, rank = blocks * blk, up.shape[0]
    piece = pltpu.VMEM(x.shape, BF16)
    slots = (peers, CAP, blk, width)
    up3 = (peers, rank // peers, width)
    ups, downs = pltpu.VMEM(up3, BF16), pltpu.VMEM(down.shape, BF16)
    links = pltpu.VMEM((peers * blocks, peers * blocks), BF16)
    return pl.pallas_call(
        functools.partial(section_kernel, sections, peers),
        name="section_layer",
        in_specs=[smem, vmem] + [hbm] * 5,
        out_specs=[vmem] * 5,
        out_shape=[
            pltpu.VMEM(x.shape, BF16),
            pltpu.VMEM(slots, BF16),
            pltpu.VMEM(up3, F32),
            pltpu.VMEM(down.shape, F32),
            pltpu.VMEM((8, 128), jnp.int32),
        ],
        scratch_shapes=[piece, piece, downs, pltpu.VMEM(up.shape, BF16)]
        + [piece] * 8
        + [
            pltpu.VMEM((rows, width), BF16), pltpu.VMEM((rows, width), F32),
            piece, piece, pltpu.VMEM(slots, BF16),
            ups, downs, links, links,
            pltpu.SMEM((peers, peers), jnp.int32),
            pltpu.VMEM((2, peers, peers), jnp.int32),
            pltpu.SemaphoreType.REGULAR,
            dma((8,)),
        ]
        + [dma((2, peers))] * 6,
        compiler_params=pltpu.CompilerParams(
            collective_id=0, has_side_effects=True, vmem_limit_bytes=48 * 1024 * 1024
        ),
    )(masks, g, wiring, x, dy, down, up)


def settle_kernel(
    wiring, place, fwd, back, up, down, next_out, ret_out, gdown_out, gup_out,
    counts, places, count_sem, row_sem, sum_sem,
):
    me = lax.axis_index("peer")
    peers = counts.shape[0]
    tables = [
        pltpu.make_async_copy(wiring.at[lax.axis_index("section")], counts, count_sem.at[0]),
        pltpu.make_async_copy(place, places, count_sem.at[1]),
    ]
    sums = [
        pltpu.make_async_copy(up, gup_out, sum_sem.at[0]),
        pltpu.make_async_copy(down, gdown_out, sum_sem.at[1]),
    ]
    for copy in tables + sums:
        copy.start()
    for copy in tables:
        copy.wait()

    def gather(p, start):
        pltpu.make_async_copy(fwd.at[places[0, p]], next_out.at[p], row_sem.at[0, p]).start()
        n = counts[me, p]
        for slot in range(CAP):
            @pl.when(slot < n)
            def _():
                at = start + slot
                pltpu.make_async_copy(back.at[p, slot], ret_out.at[at], row_sem.at[1, at]).start()

        return start + n

    lax.fori_loop(0, peers, gather, jnp.int32(0))

    @pl.loop(0, peers)
    def _(p):
        pltpu.make_async_copy(fwd.at[p], next_out.at[p], row_sem.at[0, p]).wait()
        pltpu.make_async_copy(back.at[p, 0], ret_out.at[p], row_sem.at[1, p]).wait()

    for copy in sums:
        copy.wait()


def settle(wiring, place, fwd, back, up, down):
    hbm = pl.BlockSpec(memory_space=pl.ANY)
    vmem = pl.BlockSpec(memory_space=pltpu.VMEM)
    dma = pltpu.SemaphoreType.DMA
    peers = fwd.shape[0]
    return pl.pallas_call(
        settle_kernel,
        name="settle",
        in_specs=[hbm] + [vmem] * 5,
        out_specs=[hbm] * 4,
        out_shape=[
            jax.ShapeDtypeStruct(fwd.shape, BF16),
            jax.ShapeDtypeStruct(fwd.shape, BF16),
            jax.ShapeDtypeStruct(down.shape, F32),
            jax.ShapeDtypeStruct(up.shape, F32),
        ],
        scratch_shapes=[
            pltpu.SMEM((peers, peers), jnp.int32),
            pltpu.SMEM(place.shape, jnp.int32),
            dma((2,)), dma((2, peers)), dma((2,)),
        ],
        compiler_params=pltpu.CompilerParams(vmem_limit_bytes=16 * 1024 * 1024),
    )(wiring, *(pltpu.with_memory_space_constraint(a, pltpu.VMEM) for a in (place, fwd, back, up, down)))


def body(inputs, out_grad, gains, down_proj, up_proj, wiring, pair_mask):
    sections = lax.axis_size("section")
    peers = lax.axis_size("peer")
    rows, width = inputs.shape[2:]
    rank = down_proj.shape[2]
    pieces = (peers, rows // peers, width)
    fwd, back, up, down, place = run_section(
        pair_mask, gains, wiring, inputs.reshape(pieces), out_grad.reshape(pieces),
        down_proj[0], up_proj[0], sections, peers,
    )
    next_rows, return_rows, grad_down, grad_up = settle(wiring, place, fwd, back, up, down)
    return (
        next_rows.reshape(1, 1, rows, width),
        return_rows.reshape(1, 1, rows, width),
        grad_down.reshape(1, 1, width, rank),
        grad_up.reshape(1, 1, rank, width),
    )


def solution(mesh):
    placed = (
        P("section", "peer", None, None),
        P("section", "peer", None, None),
        P("section", None),
        P("section", None, None),
        P("section", None, None),
        P(),
        P(),
    )
    return jax.shard_map(
        body,
        mesh=mesh,
        in_specs=placed,
        out_specs=(
            P("section", "peer", None, None),
            P("section", "peer", None, None),
            P("section", "peer", None, None),
            P("section", "peer", None, None),
        ),
        check_vma=False,
    )
```

```python
import functools

import jax
import jax.numpy as jnp
from jax import lax
from jax.experimental import pallas as pl
from jax.experimental.pallas import tpu as pltpu
from jax.sharding import PartitionSpec as P

CAP = 2
WIDE = 512
EARLY = 6
MESH = pl.DeviceIdType.MESH
F32, BF16 = jnp.float32, jnp.bfloat16


def dims(a, b):
    return (((a,), (b,)), ((), ()))


def mul(a, b, ca=1, cb=0):
    return lax.dot_general(a, b, dims(ca, cb), preferred_element_type=F32)


def hot(mask):
    return mask.astype(F32).astype(BF16)


def iota(shape, dim):
    return lax.broadcasted_iota(jnp.int32, shape, dim)


def block_graph(counts):
    n = counts.shape[0]
    e, bits = n * n, n.bit_length() - 1
    c = counts.astype(BF16)
    start = mul(c, hot(iota((n, n), 0) < iota((n, n), 1)))
    above = mul(hot(iota((n, n), 1) < iota((n, n), 0)), c)
    right = hot((iota((e, n), 0) >> bits) == iota((e, n), 1))
    left = hot((iota((n, e), 1) >> bits) == iota((n, e), 0))

    def grow(m):
        return mul(mul(right, m.astype(BF16), 1, 1).astype(BF16), left)

    rank = (iota((e, e), 1) & (n - 1)).astype(F32) - grow(start)
    place = (iota((e, e), 0) & (n - 1)).astype(F32)
    inside = (rank >= 0) & (rank < grow(counts)) & (place == grow(above) + rank)
    return hot(inside)


def halve(graph, left, right, size):
    e = graph.shape[0]
    row, col = iota((e, e), 0), iota((e, e), 1)
    swap = hot((row >> 1 == col >> 1) & (row != col))
    mate = mul(graph, mul(swap, graph).astype(BF16), 0, 0).astype(BF16)
    step = mul(mate, swap).astype(BF16)

    def jump(_, carry):
        low, step = carry
        low = jnp.minimum(low, mul(low.astype(BF16), step))
        return low, mul(step, step).astype(BF16)

    longest = e * size >> (e.bit_length() - 1) // 2 + 1
    low, _ = lax.fori_loop(0, longest.bit_length() - 1, jump, (iota((8, e), 1).astype(F32), step))
    side = (low > mul(low.astype(BF16), swap)).astype(F32)
    at = iota((8, e), 1)
    base = ((at & ~(size - 1)) + ((at & (size - 1)) >> 1)).astype(F32)

    def moved(half):
        return hot(row.astype(F32) == (base + half * (size // 2))[0:1, :])

    on_left, on_right = moved(side), moved(mul(side.astype(BF16), graph, 1, 1))
    graph = mul(mul(on_right, graph).astype(BF16), on_left, 1, 1).astype(BF16)
    return graph, mul(on_left, left).astype(BF16), mul(on_right, right).astype(BF16)


def colours(counts):
    graph = block_graph(counts)
    size, e = counts.shape[0], graph.shape[0]
    left = right = hot(iota((e, e), 0) == iota((e, e), 1))
    while size > 1:
        graph, left, right = halve(graph, left, right, size)
        size //= 2
    return graph, left, right


def cut(matrix, blocks, blk, rows_at, cols_at):
    e, n, bits = matrix.shape[0], blocks * blk, blk.bit_length() - 1
    pick = hot(iota((n, e), 1) == rows_at(iota((n, e), 0) >> bits))
    take = hot(iota((e, n), 0) == cols_at(iota((e, n), 1) >> bits))
    found = mul(mul(pick, matrix).astype(BF16), take)
    same = (iota((n, n), 0) & (blk - 1)) == (iota((n, n), 1) & (blk - 1))
    return hot(same & (found > 0.5))


def section_kernel(
    sections, peers, masks_in, gains, wiring, x_hbm, dy_hbm, down_hbm, up_hbm,
    fwd_out, back_out, gup_out, gdown_out, place_out,
    x_own, dy_own, down_ref, up_ref, x_pack, x_got, dy_got, x_send, dy_send, x_pair, dy_pair,
    x_flat, normed, dns, dxs, fwd, back, gup, gdown, graph_ref, left_ref,
    masks, g_ref, counts, tables, near, load_sem, x1, dy1, x2, dy2, sems_f, sems_b,
):
    section = lax.axis_index("section")
    me = lax.axis_index("peer")
    after = lax.rem(section + 1, sections)
    ahead = lax.rem(section + sections - 1, sections)
    blocks, blk, width = x_own.shape
    rows = blocks * blk
    rank = up_ref.shape[0]
    chunks = width // WIDE

    def turn(t):
        half = (t + 1) // 2
        step = half + (1 - t % 2) * (peers - 2 * half)
        return lax.rem(me + step, peers)

    loads = [
        pltpu.make_async_copy(src, dst, load_sem.at[i])
        for i, (src, dst) in enumerate((
            (x_hbm, x_own),
            (dy_hbm, dy_own),
            (down_hbm, down_ref),
            (up_hbm, up_ref),
            (wiring.at[ahead], counts),
            (wiring.at[section], tables.at[0]),
            (wiring.at[ahead], tables.at[1]),
            (dy_hbm.at[me], dy_got.at[me]),
            (masks_in, masks),
            (gains, g_ref),
        ))
    ]
    barrier = pltpu.get_barrier_semaphore()

    for where in (after, ahead):
        pl.semaphore_signal(
            barrier, inc=1, device_id={"section": where, "peer": me}, device_id_type=MESH
        )

    def greet(semaphore):
        @pl.loop(1, peers)
        def _(t):
            pl.semaphore_signal(
                semaphore, inc=1, device_id={"section": section, "peer": turn(t)}, device_id_type=MESH
            )

    greet(barrier)
    for copy in loads:
        copy.start()
    pl.semaphore_wait(barrier, peers + 1)

    def remote(src, dst, sems, where, who):
        return pltpu.make_async_remote_copy(
            src_ref=src.at[who],
            dst_ref=dst.at[me],
            send_sem=sems.at[0, who],
            recv_sem=sems.at[1, me],
            device_id={"section": where, "peer": who},
            device_id_type=MESH,
        )

    def arrival(src, dst, sems, where, who):
        return pltpu.make_async_remote_copy(
            src_ref=src.at[who],
            dst_ref=dst.at[who],
            send_sem=sems.at[0, who],
            recv_sem=sems.at[1, who],
            device_id={"section": where, "peer": who},
            device_id_type=MESH,
        )

    @pl.loop(1, peers)
    def _(t):
        remote(dy_hbm, dy_got, dy1, section, turn(t)).start()

    greet(near)

    for copy in loads:
        copy.wait()

    def cols(c):
        return pl.ds(pl.multiple_of(c * WIDE, WIDE), WIDE)

    def wide(ref, at):
        return ref[:, :, at].astype(F32).reshape(rows, WIDE)

    def tall(value):
        return value.reshape(blocks, blk, WIDE).astype(BF16)

    def inverse(x_ref):
        def squares(c, total):
            xc = wide(x_ref, cols(c))
            return total + jnp.sum(xc * xc, axis=1, keepdims=True)

        ms = lax.fori_loop(0, chunks, squares, jnp.zeros((rows, 1), F32)) / width
        return lax.rsqrt(ms + 1e-05)

    def project(x_ref, rinv, at):
        nc = (wide(x_ref, at) * rinv * g_ref[:, at]).astype(BF16)
        return nc, jnp.dot(nc, down_ref[at, :], preferred_element_type=F32)

    zero = jnp.zeros((rows, rank), F32)

    def head(x_ref, dy_ref):
        rinv = inverse(x_ref)

        def both(c, carry):
            pre, dact = carry
            at = cols(c)
            nc, part = project(x_ref, rinv, at)
            normed[:, at] = nc
            dact = dact + mul(wide(dy_ref, at).astype(BF16), up_ref[:, at], 1, 1)
            return pre + part, dact

        pre, dact = lax.fori_loop(0, chunks, both, (zero, zero))
        sig = jax.nn.sigmoid(pre)
        act = (pre * sig).astype(BF16)
        dpre = (dact * sig * (1.0 + pre * (1.0 - sig))).astype(BF16)
        return rinv, act, dpre

    def gradients(at, dy_ref, act, dpre):
        up_part = tall(mul(act, wide(dy_ref, at).astype(BF16), 0, 0))
        return up_part, mul(normed[:, at], dpre, 0, 0).astype(BF16)

    rinv, act, dpre = head(x_own, dy_own)

    def tail(c, inner):
        at = cols(c)
        dn = mul(dpre, down_ref[at, :], 1, 1) * g_ref[:, at]
        dns[:, at] = dn
        return inner + jnp.sum(dn * wide(x_own, at), axis=1, keepdims=True)

    inner = lax.fori_loop(0, chunks, tail, jnp.zeros((rows, 1), F32)) / width
    pull = rinv * rinv * inner

    @pl.loop(0, chunks)
    def _(c):
        at = cols(c)
        dxs[:, :, at] = tall(wide(dy_own, at) + rinv * (dns[:, at] - wide(x_own, at) * pull))

    def spread(q, start):
        for slot in range(CAP):
            back[q, slot] = dxs[jnp.minimum(start + slot, blocks - 1)]
        return start + counts[q, me]

    lax.fori_loop(0, peers, spread, jnp.int32(0))
    pl.semaphore_wait(near, peers - 1)

    @pl.loop(0, EARLY)
    def _(t):
        remote(back, back_out, sems_b, ahead, turn(t)).start()

    @pl.loop(0, chunks)
    def _(c):
        at = cols(c)
        gup[:, :, at], gdown[at, :] = gradients(at, dy_own, act, dpre)

    mask = masks[section]
    graph, left, _ = colours(tables[0].astype(F32))
    graph_ref[...] = graph
    left_ref[...] = left

    def order(peer):
        return cut(
            left_ref[...], blocks, blk, lambda k: peer * peers + k, lambda b: peer * peers + b
        )

    mine = order(me)

    @pl.loop(0, chunks)
    def _(c):
        at = cols(c)
        x_pack[:, :, at] = tall(mul(mine, wide(x_own, at).astype(BF16)))

    x_got[me] = x_pack[me]

    @pl.loop(1, peers)
    def _(t):
        remote(x_pack, x_got, x1, section, turn(t)).start()

    @pl.loop(1, peers)
    def _(t):
        arrival(dy_hbm, dy_got, dy1, section, turn(t)).wait_recv()

    @pl.loop(0, peers)
    def _(p):
        dy_send[p] = dy_got[jnp.bitwise_xor(p, mask)]

    dy_pair[me] = dy_send[me]

    @pl.loop(1, peers)
    def _(t):
        remote(dy_send, dy_pair, dy2, section, turn(t)).start()

    _, _, right = colours(tables[1].astype(F32))
    e = right.shape[0]
    spots = iota((8, e), 1) - me * peers
    value = jnp.where((spots >= 0) & (spots < peers), spots, 0).astype(F32)
    found = mul(value.astype(BF16), right).astype(BF16)
    lanes = place_out.shape[1]
    near = hot(iota((e, lanes), 0) - me * peers == iota((e, lanes), 1))
    place_out[...] = (mul(found, near) + 0.5).astype(jnp.int32)

    @pl.loop(1, peers)
    def _(t):
        arrival(x_pack, x_got, x1, section, turn(t)).wait_recv()

    @pl.loop(0, peers)
    def _(p):
        x_send[p] = x_got[jnp.bitwise_xor(p, mask)]

    x_pair[me] = x_send[me]

    @pl.loop(1, peers)
    def _(t):
        remote(x_send, x_pair, x2, section, turn(t)).start()

    @pl.loop(EARLY, peers)
    def _(t):
        remote(back, back_out, sems_b, ahead, turn(t)).start()

    rinv_got = inverse(x_got)
    pre_got = lax.fori_loop(
        0, chunks, lambda c, pre: pre + project(x_got, rinv_got, cols(c))[1], zero
    )
    act_got = (pre_got * jax.nn.sigmoid(pre_got)).astype(BF16)
    sorting = cut(
        graph_ref[...], blocks, blk, lambda q: q * peers + me, lambda p: p * peers + me
    )

    @pl.loop(0, chunks)
    def _(c):
        at = cols(c)
        oc = (wide(x_got, at) + mul(act_got, up_ref[:, at])).astype(BF16)
        fwd[:, :, at] = tall(mul(sorting, oc))

    @pl.loop(0, peers)
    def _(t):
        remote(fwd, fwd_out, sems_f, after, turn(t)).start()

    theirs = order(jnp.bitwise_xor(me, mask))

    @pl.loop(1, peers)
    def _(t):
        who = turn(t)
        arrival(dy_send, dy_pair, dy2, section, who).wait_recv()
        arrival(x_send, x_pair, x2, section, who).wait_recv()

    @pl.loop(0, chunks)
    def _(c):
        at = cols(c)
        x_flat[:, :, at] = tall(mul(theirs, wide(x_pair, at).astype(BF16), 0, 0))

    _, act2, dpre2 = head(x_flat, dy_pair)

    @pl.loop(0, chunks)
    def _(c):
        at = cols(c)
        up_part, down_part = gradients(at, dy_pair, act2, dpre2)
        gup_out[:, :, at] = (gup[:, :, at].astype(F32) + up_part.astype(F32)) * 0.5
        gdown_out[at, :] = (gdown[at, :].astype(F32) + down_part.astype(F32)) * 0.5

    @pl.loop(1, peers)
    def _(t):
        who = turn(t)
        remote(dy_hbm, dy_got, dy1, section, who).wait_send()
        remote(x_pack, x_got, x1, section, who).wait_send()
        remote(dy_send, dy_pair, dy2, section, who).wait_send()
        remote(x_send, x_pair, x2, section, who).wait_send()

    @pl.loop(0, peers)
    def _(t):
        who = turn(t)
        remote(fwd, fwd_out, sems_f, after, who).wait_send()
        remote(back, back_out, sems_b, ahead, who).wait_send()
        arrival(back, back_out, sems_b, ahead, who).wait_recv()
        arrival(fwd, fwd_out, sems_f, after, who).wait_recv()


def run_section(masks, g, wiring, x, dy, down, up, sections, peers):
    vmem = pl.BlockSpec(memory_space=pltpu.VMEM)
    hbm = pl.BlockSpec(memory_space=pl.ANY)
    dma = pltpu.SemaphoreType.DMA
    blocks, blk, width = x.shape
    rows, rank = blocks * blk, up.shape[0]
    piece = pltpu.VMEM(x.shape, BF16)
    slots = (peers, CAP, blk, width)
    up3 = (peers, rank // peers, width)
    ups, downs = pltpu.VMEM(up3, BF16), pltpu.VMEM(down.shape, BF16)
    links = pltpu.VMEM((peers * blocks, peers * blocks), BF16)
    return pl.pallas_call(
        functools.partial(section_kernel, sections, peers),
        name="section_layer",
        in_specs=[hbm] * 7,
        out_specs=[vmem] * 5,
        out_shape=[
            pltpu.VMEM(x.shape, BF16),
            pltpu.VMEM(slots, BF16),
            pltpu.VMEM(up3, F32),
            pltpu.VMEM(down.shape, F32),
            pltpu.VMEM((8, 128), jnp.int32),
        ],
        scratch_shapes=[piece, piece, downs, pltpu.VMEM(up.shape, BF16)]
        + [piece] * 8
        + [
            pltpu.VMEM((rows, width), BF16), pltpu.VMEM((rows, width), F32),
            piece, piece, pltpu.VMEM(slots, BF16),
            ups, downs, links, links,
            pltpu.SMEM(masks.shape, jnp.int32),
            pltpu.VMEM(g.shape, F32),
            pltpu.SMEM((peers, peers), jnp.int32),
            pltpu.VMEM((2, peers, peers), jnp.int32),
            pltpu.SemaphoreType.REGULAR,
            dma((10,)),
        ]
        + [dma((2, peers))] * 6,
        compiler_params=pltpu.CompilerParams(
            collective_id=0, has_side_effects=True, vmem_limit_bytes=48 * 1024 * 1024
        ),
    )(masks, g, wiring, x, dy, down, up)


def settle_kernel(
    wiring, place, fwd, back, up, down, next_out, ret_out, gdown_out, gup_out,
    counts, places, count_sem, row_sem, sum_sem,
):
    me = lax.axis_index("peer")
    peers = counts.shape[0]
    tables = [
        pltpu.make_async_copy(wiring.at[lax.axis_index("section")], counts, count_sem.at[0]),
        pltpu.make_async_copy(place, places, count_sem.at[1]),
    ]
    sums = [
        pltpu.make_async_copy(up, gup_out, sum_sem.at[0]),
        pltpu.make_async_copy(down, gdown_out, sum_sem.at[1]),
    ]
    for copy in tables + sums:
        copy.start()
    for copy in tables:
        copy.wait()

    def gather(p, start):
        pltpu.make_async_copy(fwd.at[places[0, p]], next_out.at[p], row_sem.at[0, p]).start()
        n = counts[me, p]
        for slot in range(CAP):
            @pl.when(slot < n)
            def _():
                at = start + slot
                pltpu.make_async_copy(back.at[p, slot], ret_out.at[at], row_sem.at[1, at]).start()

        return start + n

    lax.fori_loop(0, peers, gather, jnp.int32(0))

    @pl.loop(0, peers)
    def _(p):
        pltpu.make_async_copy(fwd.at[p], next_out.at[p], row_sem.at[0, p]).wait()
        pltpu.make_async_copy(back.at[p, 0], ret_out.at[p], row_sem.at[1, p]).wait()

    for copy in sums:
        copy.wait()


def settle(wiring, place, fwd, back, up, down):
    hbm = pl.BlockSpec(memory_space=pl.ANY)
    vmem = pl.BlockSpec(memory_space=pltpu.VMEM)
    dma = pltpu.SemaphoreType.DMA
    peers = fwd.shape[0]
    return pl.pallas_call(
        settle_kernel,
        name="settle",
        in_specs=[hbm] + [vmem] * 5,
        out_specs=[hbm] * 4,
        out_shape=[
            jax.ShapeDtypeStruct(fwd.shape, BF16),
            jax.ShapeDtypeStruct(fwd.shape, BF16),
            jax.ShapeDtypeStruct(down.shape, F32),
            jax.ShapeDtypeStruct(up.shape, F32),
        ],
        scratch_shapes=[
            pltpu.SMEM((peers, peers), jnp.int32),
            pltpu.SMEM(place.shape, jnp.int32),
            dma((2,)), dma((2, peers)), dma((2,)),
        ],
        compiler_params=pltpu.CompilerParams(vmem_limit_bytes=16 * 1024 * 1024),
    )(wiring, *(pltpu.with_memory_space_constraint(a, pltpu.VMEM) for a in (place, fwd, back, up, down)))


def body(inputs, out_grad, gains, down_proj, up_proj, wiring, pair_mask):
    sections = lax.axis_size("section")
    peers = lax.axis_size("peer")
    rows, width = inputs.shape[2:]
    rank = down_proj.shape[2]
    pieces = (peers, rows // peers, width)
    fwd, back, up, down, place = run_section(
        pair_mask, gains, wiring, inputs.reshape(pieces), out_grad.reshape(pieces),
        down_proj[0], up_proj[0], sections, peers,
    )
    next_rows, return_rows, grad_down, grad_up = settle(wiring, place, fwd, back, up, down)
    return (
        next_rows.reshape(1, 1, rows, width),
        return_rows.reshape(1, 1, rows, width),
        grad_down.reshape(1, 1, width, rank),
        grad_up.reshape(1, 1, rank, width),
    )


def solution(mesh):
    placed = (
        P("section", "peer", None, None),
        P("section", "peer", None, None),
        P("section", None),
        P("section", None, None),
        P("section", None, None),
        P(),
        P(),
    )
    return jax.shard_map(
        body,
        mesh=mesh,
        in_specs=placed,
        out_specs=(
            P("section", "peer", None, None),
            P("section", "peer", None, None),
            P("section", "peer", None, None),
            P("section", "peer", None, None),
        ),
        check_vma=False,
    )
```

```python
import functools

import jax
import jax.numpy as jnp
from jax import lax
from jax.experimental import pallas as pl
from jax.experimental.pallas import tpu as pltpu
from jax.sharding import PartitionSpec as P

CAP = 2
WIDE = 512
EARLY = 6
LATE = 11
MESH = pl.DeviceIdType.MESH
F32, BF16 = jnp.float32, jnp.bfloat16


def dims(a, b):
    return (((a,), (b,)), ((), ()))


def mul(a, b, ca=1, cb=0):
    return lax.dot_general(a, b, dims(ca, cb), preferred_element_type=F32)


def hot(mask):
    return mask.astype(F32).astype(BF16)


def iota(shape, dim):
    return lax.broadcasted_iota(jnp.int32, shape, dim)


def block_graph(counts):
    n = counts.shape[0]
    e, bits = n * n, n.bit_length() - 1
    c = counts.astype(BF16)
    start = mul(c, hot(iota((n, n), 0) < iota((n, n), 1)))
    above = mul(hot(iota((n, n), 1) < iota((n, n), 0)), c)
    right = hot((iota((e, n), 0) >> bits) == iota((e, n), 1))
    left = hot((iota((n, e), 1) >> bits) == iota((n, e), 0))

    def grow(m):
        return mul(mul(right, m.astype(BF16), 1, 1).astype(BF16), left)

    rank = (iota((e, e), 1) & (n - 1)).astype(F32) - grow(start)
    place = (iota((e, e), 0) & (n - 1)).astype(F32)
    inside = (rank >= 0) & (rank < grow(counts)) & (place == grow(above) + rank)
    return hot(inside)


def halve(graph, left, right, size):
    e = graph.shape[0]
    row, col = iota((e, e), 0), iota((e, e), 1)
    swap = hot((row >> 1 == col >> 1) & (row != col))
    mate = mul(graph, mul(swap, graph).astype(BF16), 0, 0).astype(BF16)
    step = mul(mate, swap).astype(BF16)

    def jump(_, carry):
        low, step = carry
        low = jnp.minimum(low, mul(low.astype(BF16), step))
        return low, mul(step, step).astype(BF16)

    longest = e * size >> (e.bit_length() - 1) // 2 + 1
    low, _ = lax.fori_loop(0, longest.bit_length() - 1, jump, (iota((8, e), 1).astype(F32), step))
    side = (low > mul(low.astype(BF16), swap)).astype(F32)
    at = iota((8, e), 1)
    base = ((at & ~(size - 1)) + ((at & (size - 1)) >> 1)).astype(F32)

    def moved(half):
        return hot(row.astype(F32) == (base + half * (size // 2))[0:1, :])

    on_left, on_right = moved(side), moved(mul(side.astype(BF16), graph, 1, 1))
    graph = mul(mul(on_right, graph).astype(BF16), on_left, 1, 1).astype(BF16)
    return graph, mul(on_left, left).astype(BF16), mul(on_right, right).astype(BF16)


def colours(counts):
    graph = block_graph(counts)
    size, e = counts.shape[0], graph.shape[0]
    left = right = hot(iota((e, e), 0) == iota((e, e), 1))
    while size > 1:
        graph, left, right = halve(graph, left, right, size)
        size //= 2
    return graph, left, right


def cut(matrix, blocks, blk, rows_at, cols_at):
    e, n, bits = matrix.shape[0], blocks * blk, blk.bit_length() - 1
    pick = hot(iota((n, e), 1) == rows_at(iota((n, e), 0) >> bits))
    take = hot(iota((e, n), 0) == cols_at(iota((e, n), 1) >> bits))
    found = mul(mul(pick, matrix).astype(BF16), take)
    same = (iota((n, n), 0) & (blk - 1)) == (iota((n, n), 1) & (blk - 1))
    return hot(same & (found > 0.5))


def section_kernel(
    sections, peers, masks_in, gains, wiring, x_hbm, dy_hbm, down_hbm, up_hbm,
    fwd_out, back_out, gup_out, gdown_out, place_out,
    x_own, dy_own, down_ref, up_ref, x_pack, x_got, dy_got, x_send, dy_send, x_pair, dy_pair,
    x_flat, normed, dns, dxs, fwd, back, gup, gdown, graph_ref, left_ref,
    masks, g_ref, counts, tables, near, load_sem, x1, dy1, x2, dy2, sems_f, sems_b,
):
    section = lax.axis_index("section")
    me = lax.axis_index("peer")
    after = lax.rem(section + 1, sections)
    ahead = lax.rem(section + sections - 1, sections)
    blocks, blk, width = x_own.shape
    rows = blocks * blk
    rank = up_ref.shape[0]
    chunks = width // WIDE

    def turn(t):
        half = (t + 1) // 2
        step = half + (1 - t % 2) * (peers - 2 * half)
        return lax.rem(me + step, peers)

    loads = [
        pltpu.make_async_copy(src, dst, load_sem.at[i])
        for i, (src, dst) in enumerate((
            (x_hbm, x_own),
            (dy_hbm, dy_own),
            (down_hbm, down_ref),
            (up_hbm, up_ref),
            (wiring.at[ahead], counts),
            (wiring.at[section], tables.at[0]),
            (wiring.at[ahead], tables.at[1]),
            (dy_hbm.at[me], dy_got.at[me]),
            (masks_in, masks),
            (gains, g_ref),
        ))
    ]
    barrier = pltpu.get_barrier_semaphore()

    for where in (after, ahead):
        pl.semaphore_signal(
            barrier, inc=1, device_id={"section": where, "peer": me}, device_id_type=MESH
        )

    def greet(semaphore):
        @pl.loop(1, peers)
        def _(t):
            pl.semaphore_signal(
                semaphore, inc=1, device_id={"section": section, "peer": turn(t)}, device_id_type=MESH
            )

    greet(barrier)
    for copy in loads:
        copy.start()
    pl.semaphore_wait(barrier, peers + 1)

    def remote(src, dst, sems, where, who):
        return pltpu.make_async_remote_copy(
            src_ref=src.at[who],
            dst_ref=dst.at[me],
            send_sem=sems.at[0, who],
            recv_sem=sems.at[1, me],
            device_id={"section": where, "peer": who},
            device_id_type=MESH,
        )

    def arrival(src, dst, sems, where, who):
        return pltpu.make_async_remote_copy(
            src_ref=src.at[who],
            dst_ref=dst.at[who],
            send_sem=sems.at[0, who],
            recv_sem=sems.at[1, who],
            device_id={"section": where, "peer": who},
            device_id_type=MESH,
        )

    @pl.loop(1, peers)
    def _(t):
        remote(dy_hbm, dy_got, dy1, section, turn(t)).start()

    greet(near)

    for copy in loads:
        copy.wait()

    def cols(c):
        return pl.ds(pl.multiple_of(c * WIDE, WIDE), WIDE)

    def wide(ref, at):
        return ref[:, :, at].astype(F32).reshape(rows, WIDE)

    def tall(value):
        return value.reshape(blocks, blk, WIDE).astype(BF16)

    def inverse(x_ref):
        def squares(c, total):
            xc = wide(x_ref, cols(c))
            return total + jnp.sum(xc * xc, axis=1, keepdims=True)

        ms = lax.fori_loop(0, chunks, squares, jnp.zeros((rows, 1), F32)) / width
        return lax.rsqrt(ms + 1e-05)

    def project(x_ref, rinv, at):
        nc = (wide(x_ref, at) * rinv * g_ref[:, at]).astype(BF16)
        return nc, jnp.dot(nc, down_ref[at, :], preferred_element_type=F32)

    zero = jnp.zeros((rows, rank), F32)

    def head(x_ref, dy_ref):
        rinv = inverse(x_ref)

        def both(c, carry):
            pre, dact = carry
            at = cols(c)
            nc, part = project(x_ref, rinv, at)
            normed[:, at] = nc
            dact = dact + mul(wide(dy_ref, at).astype(BF16), up_ref[:, at], 1, 1)
            return pre + part, dact

        pre, dact = lax.fori_loop(0, chunks, both, (zero, zero))
        sig = jax.nn.sigmoid(pre)
        act = (pre * sig).astype(BF16)
        dpre = (dact * sig * (1.0 + pre * (1.0 - sig))).astype(BF16)
        return rinv, act, dpre

    def gradients(at, dy_ref, act, dpre):
        up_part = tall(mul(act, wide(dy_ref, at).astype(BF16), 0, 0))
        return up_part, mul(normed[:, at], dpre, 0, 0).astype(BF16)

    rinv, act, dpre = head(x_own, dy_own)

    def tail(c, inner):
        at = cols(c)
        dn = mul(dpre, down_ref[at, :], 1, 1) * g_ref[:, at]
        dns[:, at] = dn
        return inner + jnp.sum(dn * wide(x_own, at), axis=1, keepdims=True)

    inner = lax.fori_loop(0, chunks, tail, jnp.zeros((rows, 1), F32)) / width
    pull = rinv * rinv * inner

    @pl.loop(0, chunks)
    def _(c):
        at = cols(c)
        dxs[:, :, at] = tall(wide(dy_own, at) + rinv * (dns[:, at] - wide(x_own, at) * pull))

    def spread(q, start):
        for slot in range(CAP):
            back[q, slot] = dxs[jnp.minimum(start + slot, blocks - 1)]
        return start + counts[q, me]

    lax.fori_loop(0, peers, spread, jnp.int32(0))
    pl.semaphore_wait(near, peers - 1)

    @pl.loop(0, EARLY)
    def _(t):
        remote(back, back_out, sems_b, ahead, turn(t)).start()

    @pl.loop(0, chunks)
    def _(c):
        at = cols(c)
        gup[:, :, at], gdown[at, :] = gradients(at, dy_own, act, dpre)

    mask = masks[section]
    graph, left, _ = colours(tables[0].astype(F32))
    graph_ref[...] = graph
    left_ref[...] = left

    def order(peer):
        return cut(
            left_ref[...], blocks, blk, lambda k: peer * peers + k, lambda b: peer * peers + b
        )

    mine = order(me)

    @pl.loop(0, chunks)
    def _(c):
        at = cols(c)
        x_pack[:, :, at] = tall(mul(mine, wide(x_own, at).astype(BF16)))

    x_got[me] = x_pack[me]

    @pl.loop(1, peers)
    def _(t):
        remote(x_pack, x_got, x1, section, turn(t)).start()

    @pl.loop(1, peers)
    def _(t):
        arrival(dy_hbm, dy_got, dy1, section, turn(t)).wait_recv()

    @pl.loop(0, peers)
    def _(p):
        dy_send[p] = dy_got[jnp.bitwise_xor(p, mask)]

    dy_pair[me] = dy_send[me]

    @pl.loop(1, peers)
    def _(t):
        remote(dy_send, dy_pair, dy2, section, turn(t)).start()

    _, _, right = colours(tables[1].astype(F32))
    e = right.shape[0]
    spots = iota((8, e), 1) - me * peers
    value = jnp.where((spots >= 0) & (spots < peers), spots, 0).astype(F32)
    found = mul(value.astype(BF16), right).astype(BF16)
    lanes = place_out.shape[1]
    near = hot(iota((e, lanes), 0) - me * peers == iota((e, lanes), 1))
    place_out[...] = (mul(found, near) + 0.5).astype(jnp.int32)

    @pl.loop(1, peers)
    def _(t):
        arrival(x_pack, x_got, x1, section, turn(t)).wait_recv()

    @pl.loop(0, peers)
    def _(p):
        x_send[p] = x_got[jnp.bitwise_xor(p, mask)]

    x_pair[me] = x_send[me]

    @pl.loop(1, peers)
    def _(t):
        remote(x_send, x_pair, x2, section, turn(t)).start()

    @pl.loop(EARLY, LATE)
    def _(t):
        remote(back, back_out, sems_b, ahead, turn(t)).start()

    rinv_got = inverse(x_got)
    pre_got = lax.fori_loop(
        0, chunks, lambda c, pre: pre + project(x_got, rinv_got, cols(c))[1], zero
    )
    act_got = (pre_got * jax.nn.sigmoid(pre_got)).astype(BF16)
    sorting = cut(
        graph_ref[...], blocks, blk, lambda q: q * peers + me, lambda p: p * peers + me
    )

    @pl.loop(0, chunks)
    def _(c):
        at = cols(c)
        oc = (wide(x_got, at) + mul(act_got, up_ref[:, at])).astype(BF16)
        fwd[:, :, at] = tall(mul(sorting, oc))

    @pl.loop(0, LATE)
    def _(t):
        remote(fwd, fwd_out, sems_f, after, turn(t)).start()

    @pl.loop(LATE, peers)
    def _(t):
        remote(back, back_out, sems_b, ahead, turn(t)).start()
        remote(fwd, fwd_out, sems_f, after, turn(t)).start()

    theirs = order(jnp.bitwise_xor(me, mask))

    @pl.loop(1, peers)
    def _(t):
        who = turn(t)
        arrival(dy_send, dy_pair, dy2, section, who).wait_recv()
        arrival(x_send, x_pair, x2, section, who).wait_recv()

    @pl.loop(0, chunks)
    def _(c):
        at = cols(c)
        x_flat[:, :, at] = tall(mul(theirs, wide(x_pair, at).astype(BF16), 0, 0))

    _, act2, dpre2 = head(x_flat, dy_pair)

    @pl.loop(0, chunks)
    def _(c):
        at = cols(c)
        up_part, down_part = gradients(at, dy_pair, act2, dpre2)
        gup_out[:, :, at] = (gup[:, :, at].astype(F32) + up_part.astype(F32)) * 0.5
        gdown_out[at, :] = (gdown[at, :].astype(F32) + down_part.astype(F32)) * 0.5

    @pl.loop(1, peers)
    def _(t):
        who = turn(t)
        remote(dy_hbm, dy_got, dy1, section, who).wait_send()
        remote(x_pack, x_got, x1, section, who).wait_send()
        remote(dy_send, dy_pair, dy2, section, who).wait_send()
        remote(x_send, x_pair, x2, section, who).wait_send()

    @pl.loop(0, peers)
    def _(t):
        who = turn(t)
        remote(fwd, fwd_out, sems_f, after, who).wait_send()
        remote(back, back_out, sems_b, ahead, who).wait_send()
        arrival(back, back_out, sems_b, ahead, who).wait_recv()
        arrival(fwd, fwd_out, sems_f, after, who).wait_recv()


def run_section(masks, g, wiring, x, dy, down, up, sections, peers):
    vmem = pl.BlockSpec(memory_space=pltpu.VMEM)
    hbm = pl.BlockSpec(memory_space=pl.ANY)
    dma = pltpu.SemaphoreType.DMA
    blocks, blk, width = x.shape
    rows, rank = blocks * blk, up.shape[0]
    piece = pltpu.VMEM(x.shape, BF16)
    slots = (peers, CAP, blk, width)
    up3 = (peers, rank // peers, width)
    ups, downs = pltpu.VMEM(up3, BF16), pltpu.VMEM(down.shape, BF16)
    links = pltpu.VMEM((peers * blocks, peers * blocks), BF16)
    return pl.pallas_call(
        functools.partial(section_kernel, sections, peers),
        name="section_layer",
        in_specs=[hbm] * 7,
        out_specs=[vmem] * 5,
        out_shape=[
            pltpu.VMEM(x.shape, BF16),
            pltpu.VMEM(slots, BF16),
            pltpu.VMEM(up3, F32),
            pltpu.VMEM(down.shape, F32),
            pltpu.VMEM((8, 128), jnp.int32),
        ],
        scratch_shapes=[piece, piece, downs, pltpu.VMEM(up.shape, BF16)]
        + [piece] * 8
        + [
            pltpu.VMEM((rows, width), BF16), pltpu.VMEM((rows, width), F32),
            piece, piece, pltpu.VMEM(slots, BF16),
            ups, downs, links, links,
            pltpu.SMEM(masks.shape, jnp.int32),
            pltpu.VMEM(g.shape, F32),
            pltpu.SMEM((peers, peers), jnp.int32),
            pltpu.VMEM((2, peers, peers), jnp.int32),
            pltpu.SemaphoreType.REGULAR,
            dma((10,)),
        ]
        + [dma((2, peers))] * 6,
        compiler_params=pltpu.CompilerParams(
            collective_id=0, has_side_effects=True, vmem_limit_bytes=48 * 1024 * 1024
        ),
    )(masks, g, wiring, x, dy, down, up)


def settle_kernel(
    wiring, place, fwd, back, up, down, next_out, ret_out, gdown_out, gup_out,
    counts, places, count_sem, row_sem, sum_sem,
):
    me = lax.axis_index("peer")
    peers = counts.shape[0]
    tables = [
        pltpu.make_async_copy(wiring.at[lax.axis_index("section")], counts, count_sem.at[0]),
        pltpu.make_async_copy(place, places, count_sem.at[1]),
    ]
    sums = [
        pltpu.make_async_copy(up, gup_out, sum_sem.at[0]),
        pltpu.make_async_copy(down, gdown_out, sum_sem.at[1]),
    ]
    for copy in tables + sums:
        copy.start()
    for copy in tables:
        copy.wait()

    def gather(p, start):
        pltpu.make_async_copy(fwd.at[places[0, p]], next_out.at[p], row_sem.at[0, p]).start()
        n = counts[me, p]
        for slot in range(CAP):
            @pl.when(slot < n)
            def _():
                at = start + slot
                pltpu.make_async_copy(back.at[p, slot], ret_out.at[at], row_sem.at[1, at]).start()

        return start + n

    lax.fori_loop(0, peers, gather, jnp.int32(0))

    @pl.loop(0, peers)
    def _(p):
        pltpu.make_async_copy(fwd.at[p], next_out.at[p], row_sem.at[0, p]).wait()
        pltpu.make_async_copy(back.at[p, 0], ret_out.at[p], row_sem.at[1, p]).wait()

    for copy in sums:
        copy.wait()


def settle(wiring, place, fwd, back, up, down):
    hbm = pl.BlockSpec(memory_space=pl.ANY)
    vmem = pl.BlockSpec(memory_space=pltpu.VMEM)
    dma = pltpu.SemaphoreType.DMA
    peers = fwd.shape[0]
    return pl.pallas_call(
        settle_kernel,
        name="settle",
        in_specs=[hbm] + [vmem] * 5,
        out_specs=[hbm] * 4,
        out_shape=[
            jax.ShapeDtypeStruct(fwd.shape, BF16),
            jax.ShapeDtypeStruct(fwd.shape, BF16),
            jax.ShapeDtypeStruct(down.shape, F32),
            jax.ShapeDtypeStruct(up.shape, F32),
        ],
        scratch_shapes=[
            pltpu.SMEM((peers, peers), jnp.int32),
            pltpu.SMEM(place.shape, jnp.int32),
            dma((2,)), dma((2, peers)), dma((2,)),
        ],
        compiler_params=pltpu.CompilerParams(vmem_limit_bytes=16 * 1024 * 1024),
    )(wiring, *(pltpu.with_memory_space_constraint(a, pltpu.VMEM) for a in (place, fwd, back, up, down)))


def body(inputs, out_grad, gains, down_proj, up_proj, wiring, pair_mask):
    sections = lax.axis_size("section")
    peers = lax.axis_size("peer")
    rows, width = inputs.shape[2:]
    rank = down_proj.shape[2]
    pieces = (peers, rows // peers, width)
    fwd, back, up, down, place = run_section(
        pair_mask, gains, wiring, inputs.reshape(pieces), out_grad.reshape(pieces),
        down_proj[0], up_proj[0], sections, peers,
    )
    next_rows, return_rows, grad_down, grad_up = settle(wiring, place, fwd, back, up, down)
    return (
        next_rows.reshape(1, 1, rows, width),
        return_rows.reshape(1, 1, rows, width),
        grad_down.reshape(1, 1, width, rank),
        grad_up.reshape(1, 1, rank, width),
    )


def solution(mesh):
    placed = (
        P("section", "peer", None, None),
        P("section", "peer", None, None),
        P("section", None),
        P("section", None, None),
        P("section", None, None),
        P(),
        P(),
    )
    return jax.shard_map(
        body,
        mesh=mesh,
        in_specs=placed,
        out_specs=(
            P("section", "peer", None, None),
            P("section", "peer", None, None),
            P("section", "peer", None, None),
            P("section", "peer", None, None),
        ),
        check_vma=False,
    )
```

```python
import functools

import jax
import jax.numpy as jnp
from jax import lax
from jax.experimental import pallas as pl
from jax.experimental.pallas import tpu as pltpu
from jax.sharding import PartitionSpec as P

CAP = 2
WIDE = 512
EARLY = 6
MESH = pl.DeviceIdType.MESH
F32, BF16 = jnp.float32, jnp.bfloat16


def dims(a, b):
    return (((a,), (b,)), ((), ()))


def mul(a, b, ca=1, cb=0):
    return lax.dot_general(a, b, dims(ca, cb), preferred_element_type=F32)


def hot(mask):
    return mask.astype(F32).astype(BF16)


def iota(shape, dim):
    return lax.broadcasted_iota(jnp.int32, shape, dim)


def block_graph(counts):
    n = counts.shape[0]
    e, bits = n * n, n.bit_length() - 1
    c = counts.astype(BF16)
    start = mul(c, hot(iota((n, n), 0) < iota((n, n), 1)))
    above = mul(hot(iota((n, n), 1) < iota((n, n), 0)), c)
    right = hot((iota((e, n), 0) >> bits) == iota((e, n), 1))
    left = hot((iota((n, e), 1) >> bits) == iota((n, e), 0))

    def grow(m):
        return mul(mul(right, m.astype(BF16), 1, 1).astype(BF16), left)

    rank = (iota((e, e), 1) & (n - 1)).astype(F32) - grow(start)
    place = (iota((e, e), 0) & (n - 1)).astype(F32)
    inside = (rank >= 0) & (rank < grow(counts)) & (place == grow(above) + rank)
    return hot(inside)


def halve(graph, left, right, size):
    e = graph.shape[0]
    row, col = iota((e, e), 0), iota((e, e), 1)
    swap = hot((row >> 1 == col >> 1) & (row != col))
    mate = mul(graph, mul(swap, graph).astype(BF16), 0, 0).astype(BF16)
    step = mul(mate, swap).astype(BF16)

    def jump(_, carry):
        low, step = carry
        low = jnp.minimum(low, mul(low.astype(BF16), step))
        return low, mul(step, step).astype(BF16)

    longest = e * size >> (e.bit_length() - 1) // 2 + 1
    low, _ = lax.fori_loop(0, longest.bit_length() - 1, jump, (iota((8, e), 1).astype(F32), step))
    side = (low > mul(low.astype(BF16), swap)).astype(F32)
    at = iota((8, e), 1)
    base = ((at & ~(size - 1)) + ((at & (size - 1)) >> 1)).astype(F32)

    def moved(half):
        return hot(row.astype(F32) == (base + half * (size // 2))[0:1, :])

    on_left, on_right = moved(side), moved(mul(side.astype(BF16), graph, 1, 1))
    graph = mul(mul(on_right, graph).astype(BF16), on_left, 1, 1).astype(BF16)
    return graph, mul(on_left, left).astype(BF16), mul(on_right, right).astype(BF16)


def colours(counts):
    graph = block_graph(counts)
    size, e = counts.shape[0], graph.shape[0]
    left = right = hot(iota((e, e), 0) == iota((e, e), 1))
    while size > 1:
        graph, left, right = halve(graph, left, right, size)
        size //= 2
    return graph, left, right


def cut(matrix, blocks, blk, rows_at, cols_at):
    e, n, bits = matrix.shape[0], blocks * blk, blk.bit_length() - 1
    pick = hot(iota((n, e), 1) == rows_at(iota((n, e), 0) >> bits))
    take = hot(iota((e, n), 0) == cols_at(iota((e, n), 1) >> bits))
    found = mul(mul(pick, matrix).astype(BF16), take)
    same = (iota((n, n), 0) & (blk - 1)) == (iota((n, n), 1) & (blk - 1))
    return hot(same & (found > 0.5))


def section_kernel(
    sections, peers, masks_in, gains, wiring, x_hbm, dy_hbm, down_hbm, up_hbm,
    fwd_out, back_out, gup_out, gdown_out, place_out,
    x_own, dy_own, down_ref, up_ref, x_pack, x_got, dy_got, x_send, dy_send, x_pair, dy_pair,
    x_flat, normed, dns, dxs, fwd, back, gup, gdown, graph_ref, left_ref,
    masks, g_ref, counts, tables, near, load_sem, x1, dy1, x2, dy2, sems_f, sems_b,
):
    section = lax.axis_index("section")
    me = lax.axis_index("peer")
    after = lax.rem(section + 1, sections)
    ahead = lax.rem(section + sections - 1, sections)
    blocks, blk, width = x_own.shape
    rows = blocks * blk
    rank = up_ref.shape[0]
    chunks = width // WIDE

    def turn(t):
        half = (t + 1) // 2
        step = half + (1 - t % 2) * (peers - 2 * half)
        step = step + lax.rem(section, 2) * (peers - 2 * step)
        return lax.rem(me + step, peers)

    loads = [
        pltpu.make_async_copy(src, dst, load_sem.at[i])
        for i, (src, dst) in enumerate((
            (x_hbm, x_own),
            (dy_hbm, dy_own),
            (down_hbm, down_ref),
            (up_hbm, up_ref),
            (wiring.at[ahead], counts),
            (wiring.at[section], tables.at[0]),
            (wiring.at[ahead], tables.at[1]),
            (dy_hbm.at[me], dy_got.at[me]),
            (masks_in, masks),
            (gains, g_ref),
        ))
    ]
    barrier = pltpu.get_barrier_semaphore()

    for where in (after, ahead):
        pl.semaphore_signal(
            barrier, inc=1, device_id={"section": where, "peer": me}, device_id_type=MESH
        )

    def greet(semaphore):
        @pl.loop(1, peers)
        def _(t):
            pl.semaphore_signal(
                semaphore, inc=1, device_id={"section": section, "peer": turn(t)}, device_id_type=MESH
            )

    greet(barrier)
    for copy in loads:
        copy.start()
    pl.semaphore_wait(barrier, peers + 1)

    def remote(src, dst, sems, where, who):
        return pltpu.make_async_remote_copy(
            src_ref=src.at[who],
            dst_ref=dst.at[me],
            send_sem=sems.at[0, who],
            recv_sem=sems.at[1, me],
            device_id={"section": where, "peer": who},
            device_id_type=MESH,
        )

    def arrival(src, dst, sems, where, who):
        return pltpu.make_async_remote_copy(
            src_ref=src.at[who],
            dst_ref=dst.at[who],
            send_sem=sems.at[0, who],
            recv_sem=sems.at[1, who],
            device_id={"section": where, "peer": who},
            device_id_type=MESH,
        )

    @pl.loop(1, peers)
    def _(t):
        remote(dy_hbm, dy_got, dy1, section, turn(t)).start()

    greet(near)

    for copy in loads:
        copy.wait()

    def cols(c):
        return pl.ds(pl.multiple_of(c * WIDE, WIDE), WIDE)

    def wide(ref, at):
        return ref[:, :, at].astype(F32).reshape(rows, WIDE)

    def tall(value):
        return value.reshape(blocks, blk, WIDE).astype(BF16)

    def inverse(x_ref):
        def squares(c, total):
            xc = wide(x_ref, cols(c))
            return total + jnp.sum(xc * xc, axis=1, keepdims=True)

        ms = lax.fori_loop(0, chunks, squares, jnp.zeros((rows, 1), F32)) / width
        return lax.rsqrt(ms + 1e-05)

    def project(x_ref, rinv, at):
        nc = (wide(x_ref, at) * rinv * g_ref[:, at]).astype(BF16)
        return nc, jnp.dot(nc, down_ref[at, :], preferred_element_type=F32)

    zero = jnp.zeros((rows, rank), F32)

    def head(x_ref, dy_ref):
        rinv = inverse(x_ref)

        def both(c, carry):
            pre, dact = carry
            at = cols(c)
            nc, part = project(x_ref, rinv, at)
            normed[:, at] = nc
            dact = dact + mul(wide(dy_ref, at).astype(BF16), up_ref[:, at], 1, 1)
            return pre + part, dact

        pre, dact = lax.fori_loop(0, chunks, both, (zero, zero))
        sig = jax.nn.sigmoid(pre)
        act = (pre * sig).astype(BF16)
        dpre = (dact * sig * (1.0 + pre * (1.0 - sig))).astype(BF16)
        return rinv, act, dpre

    def gradients(at, dy_ref, act, dpre):
        up_part = tall(mul(act, wide(dy_ref, at).astype(BF16), 0, 0))
        return up_part, mul(normed[:, at], dpre, 0, 0).astype(BF16)

    rinv, act, dpre = head(x_own, dy_own)

    def tail(c, inner):
        at = cols(c)
        dn = mul(dpre, down_ref[at, :], 1, 1) * g_ref[:, at]
        dns[:, at] = dn
        return inner + jnp.sum(dn * wide(x_own, at), axis=1, keepdims=True)

    inner = lax.fori_loop(0, chunks, tail, jnp.zeros((rows, 1), F32)) / width
    pull = rinv * rinv * inner

    @pl.loop(0, chunks)
    def _(c):
        at = cols(c)
        dxs[:, :, at] = tall(wide(dy_own, at) + rinv * (dns[:, at] - wide(x_own, at) * pull))

    def spread(q, start):
        for slot in range(CAP):
            back[q, slot] = dxs[jnp.minimum(start + slot, blocks - 1)]
        return start + counts[q, me]

    lax.fori_loop(0, peers, spread, jnp.int32(0))
    pl.semaphore_wait(near, peers - 1)

    @pl.loop(0, EARLY)
    def _(t):
        remote(back, back_out, sems_b, ahead, turn(t)).start()

    @pl.loop(0, chunks)
    def _(c):
        at = cols(c)
        gup[:, :, at], gdown[at, :] = gradients(at, dy_own, act, dpre)

    mask = masks[section]
    graph, left, _ = colours(tables[0].astype(F32))
    graph_ref[...] = graph
    left_ref[...] = left

    def order(peer):
        return cut(
            left_ref[...], blocks, blk, lambda k: peer * peers + k, lambda b: peer * peers + b
        )

    mine = order(me)

    @pl.loop(0, chunks)
    def _(c):
        at = cols(c)
        x_pack[:, :, at] = tall(mul(mine, wide(x_own, at).astype(BF16)))

    x_got[me] = x_pack[me]

    @pl.loop(1, peers)
    def _(t):
        remote(x_pack, x_got, x1, section, turn(t)).start()

    @pl.loop(1, peers)
    def _(t):
        arrival(dy_hbm, dy_got, dy1, section, turn(t)).wait_recv()

    @pl.loop(0, peers)
    def _(p):
        dy_send[p] = dy_got[jnp.bitwise_xor(p, mask)]

    dy_pair[me] = dy_send[me]

    @pl.loop(1, peers)
    def _(t):
        remote(dy_send, dy_pair, dy2, section, turn(t)).start()

    _, _, right = colours(tables[1].astype(F32))
    e = right.shape[0]
    spots = iota((8, e), 1) - me * peers
    value = jnp.where((spots >= 0) & (spots < peers), spots, 0).astype(F32)
    found = mul(value.astype(BF16), right).astype(BF16)
    lanes = place_out.shape[1]
    near = hot(iota((e, lanes), 0) - me * peers == iota((e, lanes), 1))
    place_out[...] = (mul(found, near) + 0.5).astype(jnp.int32)

    @pl.loop(1, peers)
    def _(t):
        arrival(x_pack, x_got, x1, section, turn(t)).wait_recv()

    @pl.loop(0, peers)
    def _(p):
        x_send[p] = x_got[jnp.bitwise_xor(p, mask)]

    x_pair[me] = x_send[me]

    @pl.loop(1, peers)
    def _(t):
        remote(x_send, x_pair, x2, section, turn(t)).start()

    @pl.loop(EARLY, peers)
    def _(t):
        remote(back, back_out, sems_b, ahead, turn(t)).start()

    rinv_got = inverse(x_got)
    pre_got = lax.fori_loop(
        0, chunks, lambda c, pre: pre + project(x_got, rinv_got, cols(c))[1], zero
    )
    act_got = (pre_got * jax.nn.sigmoid(pre_got)).astype(BF16)
    sorting = cut(
        graph_ref[...], blocks, blk, lambda q: q * peers + me, lambda p: p * peers + me
    )

    @pl.loop(0, chunks)
    def _(c):
        at = cols(c)
        oc = (wide(x_got, at) + mul(act_got, up_ref[:, at])).astype(BF16)
        fwd[:, :, at] = tall(mul(sorting, oc))

    @pl.loop(0, peers)
    def _(t):
        remote(fwd, fwd_out, sems_f, after, turn(t)).start()

    theirs = order(jnp.bitwise_xor(me, mask))

    @pl.loop(1, peers)
    def _(t):
        who = turn(t)
        arrival(dy_send, dy_pair, dy2, section, who).wait_recv()
        arrival(x_send, x_pair, x2, section, who).wait_recv()

    @pl.loop(0, chunks)
    def _(c):
        at = cols(c)
        x_flat[:, :, at] = tall(mul(theirs, wide(x_pair, at).astype(BF16), 0, 0))

    _, act2, dpre2 = head(x_flat, dy_pair)

    @pl.loop(0, chunks)
    def _(c):
        at = cols(c)
        up_part, down_part = gradients(at, dy_pair, act2, dpre2)
        gup_out[:, :, at] = (gup[:, :, at].astype(F32) + up_part.astype(F32)) * 0.5
        gdown_out[at, :] = (gdown[at, :].astype(F32) + down_part.astype(F32)) * 0.5

    @pl.loop(1, peers)
    def _(t):
        who = turn(t)
        remote(dy_hbm, dy_got, dy1, section, who).wait_send()
        remote(x_pack, x_got, x1, section, who).wait_send()
        remote(dy_send, dy_pair, dy2, section, who).wait_send()
        remote(x_send, x_pair, x2, section, who).wait_send()

    @pl.loop(0, peers)
    def _(t):
        who = turn(t)
        remote(fwd, fwd_out, sems_f, after, who).wait_send()
        remote(back, back_out, sems_b, ahead, who).wait_send()
        arrival(back, back_out, sems_b, ahead, who).wait_recv()
        arrival(fwd, fwd_out, sems_f, after, who).wait_recv()


def run_section(masks, g, wiring, x, dy, down, up, sections, peers):
    vmem = pl.BlockSpec(memory_space=pltpu.VMEM)
    hbm = pl.BlockSpec(memory_space=pl.ANY)
    dma = pltpu.SemaphoreType.DMA
    blocks, blk, width = x.shape
    rows, rank = blocks * blk, up.shape[0]
    piece = pltpu.VMEM(x.shape, BF16)
    slots = (peers, CAP, blk, width)
    up3 = (peers, rank // peers, width)
    ups, downs = pltpu.VMEM(up3, BF16), pltpu.VMEM(down.shape, BF16)
    links = pltpu.VMEM((peers * blocks, peers * blocks), BF16)
    return pl.pallas_call(
        functools.partial(section_kernel, sections, peers),
        name="section_layer",
        in_specs=[hbm] * 7,
        out_specs=[vmem] * 5,
        out_shape=[
            pltpu.VMEM(x.shape, BF16),
            pltpu.VMEM(slots, BF16),
            pltpu.VMEM(up3, F32),
            pltpu.VMEM(down.shape, F32),
            pltpu.VMEM((8, 128), jnp.int32),
        ],
        scratch_shapes=[piece, piece, downs, pltpu.VMEM(up.shape, BF16)]
        + [piece] * 8
        + [
            pltpu.VMEM((rows, width), BF16), pltpu.VMEM((rows, width), F32),
            piece, piece, pltpu.VMEM(slots, BF16),
            ups, downs, links, links,
            pltpu.SMEM(masks.shape, jnp.int32),
            pltpu.VMEM(g.shape, F32),
            pltpu.SMEM((peers, peers), jnp.int32),
            pltpu.VMEM((2, peers, peers), jnp.int32),
            pltpu.SemaphoreType.REGULAR,
            dma((10,)),
        ]
        + [dma((2, peers))] * 6,
        compiler_params=pltpu.CompilerParams(
            collective_id=0, has_side_effects=True, vmem_limit_bytes=48 * 1024 * 1024
        ),
    )(masks, g, wiring, x, dy, down, up)


def settle_kernel(
    wiring, place, fwd, back, up, down, next_out, ret_out, gdown_out, gup_out,
    counts, places, count_sem, row_sem, sum_sem,
):
    me = lax.axis_index("peer")
    peers = counts.shape[0]
    tables = [
        pltpu.make_async_copy(wiring.at[lax.axis_index("section")], counts, count_sem.at[0]),
        pltpu.make_async_copy(place, places, count_sem.at[1]),
    ]
    sums = [
        pltpu.make_async_copy(up, gup_out, sum_sem.at[0]),
        pltpu.make_async_copy(down, gdown_out, sum_sem.at[1]),
    ]
    for copy in tables + sums:
        copy.start()
    for copy in tables:
        copy.wait()

    def gather(p, start):
        pltpu.make_async_copy(fwd.at[places[0, p]], next_out.at[p], row_sem.at[0, p]).start()
        n = counts[me, p]
        for slot in range(CAP):
            @pl.when(slot < n)
            def _():
                at = start + slot
                pltpu.make_async_copy(back.at[p, slot], ret_out.at[at], row_sem.at[1, at]).start()

        return start + n

    lax.fori_loop(0, peers, gather, jnp.int32(0))

    @pl.loop(0, peers)
    def _(p):
        pltpu.make_async_copy(fwd.at[p], next_out.at[p], row_sem.at[0, p]).wait()
        pltpu.make_async_copy(back.at[p, 0], ret_out.at[p], row_sem.at[1, p]).wait()

    for copy in sums:
        copy.wait()


def settle(wiring, place, fwd, back, up, down):
    hbm = pl.BlockSpec(memory_space=pl.ANY)
    vmem = pl.BlockSpec(memory_space=pltpu.VMEM)
    dma = pltpu.SemaphoreType.DMA
    peers = fwd.shape[0]
    return pl.pallas_call(
        settle_kernel,
        name="settle",
        in_specs=[hbm] + [vmem] * 5,
        out_specs=[hbm] * 4,
        out_shape=[
            jax.ShapeDtypeStruct(fwd.shape, BF16),
            jax.ShapeDtypeStruct(fwd.shape, BF16),
            jax.ShapeDtypeStruct(down.shape, F32),
            jax.ShapeDtypeStruct(up.shape, F32),
        ],
        scratch_shapes=[
            pltpu.SMEM((peers, peers), jnp.int32),
            pltpu.SMEM(place.shape, jnp.int32),
            dma((2,)), dma((2, peers)), dma((2,)),
        ],
        compiler_params=pltpu.CompilerParams(vmem_limit_bytes=16 * 1024 * 1024),
    )(wiring, *(pltpu.with_memory_space_constraint(a, pltpu.VMEM) for a in (place, fwd, back, up, down)))


def body(inputs, out_grad, gains, down_proj, up_proj, wiring, pair_mask):
    sections = lax.axis_size("section")
    peers = lax.axis_size("peer")
    rows, width = inputs.shape[2:]
    rank = down_proj.shape[2]
    pieces = (peers, rows // peers, width)
    fwd, back, up, down, place = run_section(
        pair_mask, gains, wiring, inputs.reshape(pieces), out_grad.reshape(pieces),
        down_proj[0], up_proj[0], sections, peers,
    )
    next_rows, return_rows, grad_down, grad_up = settle(wiring, place, fwd, back, up, down)
    return (
        next_rows.reshape(1, 1, rows, width),
        return_rows.reshape(1, 1, rows, width),
        grad_down.reshape(1, 1, width, rank),
        grad_up.reshape(1, 1, rank, width),
    )


def solution(mesh):
    placed = (
        P("section", "peer", None, None),
        P("section", "peer", None, None),
        P("section", None),
        P("section", None, None),
        P("section", None, None),
        P(),
        P(),
    )
    return jax.shard_map(
        body,
        mesh=mesh,
        in_specs=placed,
        out_specs=(
            P("section", "peer", None, None),
            P("section", "peer", None, None),
            P("section", "peer", None, None),
            P("section", "peer", None, None),
        ),
        check_vma=False,
    )
```
